128 devices in a mesh: blk: 64 (over y, z, x_lo, core), col: 2 (over x_hi).
Axes of the slice: x: 4 (x_hi: 2, x_lo: 2; x = x_hi * 2 + x_lo), y: 4, z: 4, core: 2. Of those that a mesh axis runs over, the one named last changes fastest.
Arguments:
- encodings: bfloat16 [32768, 1024], P(('blk', 'col')), may hold values from -8 to 8
- first_weight: bfloat16 [1024, 512], replicated, may hold values from -0.1875 to 0.1875
- second_weight: bfloat16 [512, 32], replicated, may hold values from -0.25 to 0.25
- inv_scale: float32 [32], replicated, may hold values from 0.2 to 0.8
- outputscale: float32 [1], replicated, may hold values from 0.5 to 2
- noise: float32 [1], replicated, may hold values from 0.2 to 2
- rhs: float32 [32, 32768], P('col', 'blk'), may hold values from -12 to 12
Outputs:
- solution: float32 [32, 32768], P('col', 'blk')
- residual: float32 [32, 32768], P('col', 'blk')
The draws below stay inside these ranges and needn't reach their ends.
All inputs are finite; a program needn't handle non-finite values.
Results may differ from the reference program's by a relative error of at most 0.0079.
Values sent between devices are 32-bit elements; how exact they have to be, the bound alone decides.
No kernel may reach another device: no remote copies, remote signals or barrier semaphores. Data moves between devices by JAX's collectives and lax.ppermute only.
A program may use at most 64 MiB of HBM per device.

```python
import math
import jax
import jax.numpy as jnp
from jax import lax

ENC = 1024
HID = 512
FEAT = 32
COLS = 32
ITERS = 1
PTS_DEV = 512
NPTS = 32768


def draw_rhs(key, part):
    position = jnp.arange(NPTS, dtype=jnp.float32) / NPTS
    rising = 1.0 + 2.0 * position
    values = jnp.clip(jax.random.normal(key, (COLS, NPTS), jnp.float32), -4.0, 4.0) * rising[None, :]
    return values


def steps_of(stream_key, dims, cuts, smallest, high):
    def one(dim, shards_of):
        draws = jax.random.uniform(jax.random.fold_in(jax.random.fold_in(stream_key, 6), dim), (shards_of,), jnp.float32, smallest / len(cuts), high / len(cuts))
        return jnp.repeat(jnp.exp(draws), dims[dim] // shards_of).reshape((-1,) + (1,) * (len(dims) - dim - 1))

    loudness = one(*cuts[0])
    for cut in cuts[1:]:
        loudness = loudness * one(*cut)
    return loudness


def bell_draw(stream_key, dims, deviation, bound, pieces=(), kind=jnp.bfloat16):
    array = deviation * jax.random.normal(stream_key, dims, jnp.float32)
    if pieces:
        array = array * steps_of(stream_key, dims, pieces, -0.22, 0.18)
    return jnp.clip(array, -bound, bound).astype(kind)


def setup_inputs(seed: int = 0) -> dict:
    key_of = jax.random.split(jax.random.key(seed), 8)
    encodings = bell_draw(key_of[0], (NPTS, ENC), 2.0, 8.0, ((0, 128),))
    first_weight = bell_draw(key_of[1], (ENC, HID), ENC ** -0.5, 0.1875)
    second_weight = bell_draw(key_of[2], (HID, FEAT), HID ** -0.5, 0.25)
    inv_scale = jnp.clip(jnp.exp(jax.random.uniform(key_of[3], (FEAT,), jnp.float32, math.log(0.2), math.log(0.8))), 0.2, 0.8)
    outputscale = jnp.clip(jax.random.uniform(key_of[4], (1,), jnp.float32, 0.5, 2.0), 0.5, 2.0)
    noise = jnp.clip(jnp.exp(jax.random.uniform(key_of[5], (1,), jnp.float32, math.log(0.2), math.log(2.0))), 0.2, 2.0)
    rhs = draw_rhs(jax.random.fold_in(key_of[7], 71), 0)
    return dict(encodings=encodings, first_weight=first_weight, second_weight=second_weight, inv_scale=inv_scale, outputscale=outputscale, noise=noise, rhs=rhs)


def features_of(encodings, first_weight, second_weight, inv_scale):
    hidden = jnp.maximum(jnp.dot(encodings, first_weight, preferred_element_type=jnp.float32), 0.0).astype(jnp.bfloat16)
    scaled = jnp.dot(hidden, second_weight, preferred_element_type=jnp.float32) * inv_scale[None, :]
    return scaled.T


def apply_kernel(points, vectors, kernel_scale, nugget):
    norms = jnp.sum(points * points, axis=0)
    row_groups = points.reshape(FEAT, NPTS // PTS_DEV, PTS_DEV).transpose(1, 0, 2)

    def one_group(row_points):
        cross = lax.dot_general(row_points, points, (((0,), (0,)), ((), ())), precision=lax.Precision.HIGHEST)
        distance = jnp.sum(row_points * row_points, axis=0)[:, None] + norms[None, :] - 2.0 * cross
        kernel_tile = kernel_scale * jnp.exp(-0.5 * distance)
        return lax.dot_general(vectors, kernel_tile, (((1,), (1,)), ((), ())), precision=lax.Precision.HIGHEST)

    images = lax.map(one_group, row_groups)
    return images.transpose(1, 0, 2).reshape(COLS, NPTS) + nugget * vectors


def reference(encodings, first_weight, second_weight, inv_scale, outputscale, noise, rhs):
    points = features_of(encodings, first_weight, second_weight, inv_scale)
    solution = jnp.zeros_like(rhs)
    residual = rhs
    direction = rhs
    norm_now = jnp.sum(residual * residual, axis=1)
    for sweep in range(ITERS):
        images = apply_kernel(points, direction, outputscale[0], noise[0])
        step_size = norm_now / jnp.sum(direction * images, axis=1)
        solution = solution + step_size[:, None] * direction
        residual = residual - step_size[:, None] * images
        if sweep + 1 < ITERS:
            norm_next = jnp.sum(residual * residual, axis=1)
            direction = residual + (norm_next / norm_now)[:, None] * direction
            norm_now = norm_next
    return solution, residual
```

```python
import jax
import jax.numpy as jnp
from jax import lax
from jax.experimental import pallas as pl
from jax.experimental.pallas import tpu as pltpu
from jax.sharding import Mesh
from jax.sharding import PartitionSpec as P

F32, BF16 = jnp.float32, jnp.bfloat16
ROOT_LOG2E = 1.2011224087864498
CHIPS = 32
PEERS = 64
P_SETS = 8
WIDTH = 32
DEPTH = 256


def halves(x):
    high = x.astype(BF16)
    return high, (x - high.astype(F32)).astype(BF16)


def pack_kernel(enc_ref, w1_ref, w2_ref, inv_ref, rhs_ref, out_ref, set_ref):
    hidden = jnp.maximum(
        jnp.dot(enc_ref[...], w1_ref[...], preferred_element_type=F32), 0.0
    ).astype(BF16)
    features = lax.dot_general(
        w2_ref[...], hidden, (((0,), (1,)), ((), ())), preferred_element_type=F32
    )
    n = features.shape[0]
    diagonal = lax.broadcasted_iota(jnp.int32, (n, n), 0) == lax.broadcasted_iota(
        jnp.int32, (n, n), 1
    )
    inv = jnp.sum(
        jnp.where(diagonal, jnp.broadcast_to(inv_ref[...], (n, n)), 0.0), axis=1, keepdims=True
    )
    features = features * inv * ROOT_LOG2E
    half = rhs_ref.shape[1] // 2
    for p in range(P_SETS):
        at = slice(WIDTH * p, WIDTH * (p + 1))
        late = slice(half + WIDTH * p, half + WIDTH * (p + 1))
        set_ref[p] = jnp.concatenate(
            [features[:16, at], features[16:, at], rhs_ref[:, at], rhs_ref[:, late]], axis=1
        )
    for k in range(PEERS):
        out_ref[k, :16] = set_ref[k // P_SETS]
        out_ref[k, 16:] = set_ref[k % P_SETS]


def points_of(ref, k, lo):
    a0, a1 = ref[2 * k, lo : lo + 16], ref[2 * k + 1, lo : lo + 16]
    b0, b1 = ref[CHIPS + 2 * k, lo : lo + 16], ref[CHIPS + 2 * k + 1, lo : lo + 16]
    four = (a0, b0, a1, b1)
    features = jnp.concatenate(
        [
            jnp.concatenate([x[:, :32] for x in four], axis=1),
            jnp.concatenate([x[:, 32:64] for x in four], axis=1),
        ],
        axis=0,
    )
    columns = jnp.concatenate(
        [
            jnp.concatenate([a0[:, 64:], a1[:, 64:]], axis=1),
            jnp.concatenate([b0[:, 64:], b1[:, 64:]], axis=1),
        ],
        axis=0,
    )
    return features, columns


def operand(features, left):
    y1, y2 = halves(features)
    kept = y1.astype(F32) + y2.astype(F32)
    norm = -0.5 * jnp.sum(kept * kept, axis=0, keepdims=True)
    n1 = norm.astype(BF16).astype(F32)
    n2 = (norm - n1).astype(BF16).astype(F32)
    n3 = norm - n1 - n2
    row = lax.broadcasted_iota(jnp.int32, (16, features.shape[1]), 0)
    own, other = (3, 0) if left else (0, 3)
    tail = jnp.where(
        row == own,
        n1,
        jnp.where(
            row == own + 1,
            n2,
            jnp.where(
                row == own + 2, n3, jnp.where((row >= other) & (row < other + 3), 1.0, 0.0)
            ),
        ),
    ).astype(BF16)
    blank = jnp.zeros((DEPTH - 144, features.shape[1]), BF16)
    parts = [y1, y1, y2, y2] if left else [y1, y2, y1, y2]
    return jnp.concatenate(parts + [tail, blank], axis=0)


def product_kernel(own_ref, other_ref, out_ref, left_ref, right_ref, vec_ref, rows_ref, acc_ref):
    tiles = CHIPS // 2

    def prepare(k, _):
        features, columns = points_of(own_ref, k, 0)
        at = pl.ds(pl.multiple_of(k * 128, 128), 128)
        left_ref[at, :] = operand(features, True).T
        rows_ref[k] = columns
        for n, (ref, lo) in enumerate(((own_ref, 16), (other_ref, 0))):
            features, columns = points_of(ref, k, lo)
            at = pl.ds(pl.multiple_of((n * tiles + k) * 128, 128), 128)
            right_ref[:, at] = operand(features, False)
            v1, v2 = halves(columns)
            vec_ref[at, :] = jnp.concatenate([v1, v2], axis=0).T
        return 0

    lax.fori_loop(0, tiles, prepare, 0)
    acc_ref[...] = jnp.zeros_like(acc_ref)

    def multiply(j, _):
        at = pl.ds(pl.multiple_of(j * 256, 256), 256)
        right = right_ref[:, at]
        vec = vec_ref[at, :]
        for r in range(left_ref.shape[0] // 256):
            rows = slice(256 * r, 256 * (r + 1))
            exponent = jnp.dot(left_ref[rows, :], right, preferred_element_type=F32)
            tile = jnp.exp2(exponent).astype(BF16)
            acc_ref[rows, :] += jnp.dot(tile, vec, preferred_element_type=F32)
        return 0

    lax.fori_loop(0, right_ref.shape[1] // 256, multiply, 0)

    product = jnp.zeros((32, 128), F32)
    square = jnp.zeros((32, 128), F32)
    for k in range(tiles):
        both = acc_ref[128 * k : 128 * (k + 1), :].T
        image = both[:32] + both[32:]
        rows = rows_ref[k]
        product = product + rows * image
        square = square + rows * rows
        for xh in range(2):
            top, low = image[16 * xh : 16 * xh + 8], image[16 * xh + 8 : 16 * xh + 16]
            for chip in range(2):
                at = slice(64 * chip, 64 * (chip + 1))
                out_ref[CHIPS * xh + 2 * k + chip, :8] = jnp.concatenate(
                    [top[:, at], low[:, at]], axis=1
                )
    product = jnp.sum(product, axis=1, keepdims=True)
    square = jnp.sum(square, axis=1, keepdims=True) * (P_SETS / PEERS)
    lane = lax.broadcasted_iota(jnp.int32, (8, 128), 1)
    for xh in range(2):
        sums = jnp.zeros((8, 128), F32)
        for n, x in enumerate((product, square)):
            for a in range(2):
                lo = 16 * xh + 8 * a
                sums = jnp.where(lane == 2 * n + a, x[lo : lo + 8], sums)
        out_ref[CHIPS * xh : CHIPS * (xh + 1), 8:] = jnp.broadcast_to(sums, (CHIPS, 8, 128))


def finish_kernel(got_ref, own_ref, other_ref, rhs_ref, scale_ref, noise_ref, sol_ref, res_ref):
    scale, noise = scale_ref[0], noise_ref[0]
    sums = own_ref[...] + other_ref[...]
    product = jnp.concatenate([sums[:, 0:1], sums[:, 1:2]], axis=0)
    square = jnp.concatenate([sums[:, 2:3], sums[:, 3:4]], axis=0)
    step = square / (scale * product + noise * square)
    per = PEERS // P_SETS
    parts = []
    for p in range(P_SETS):
        part = got_ref[per * p, :8]
        for q in range(1, per):
            part = part + got_ref[per * p + q, :8]
        parts.append(part)
    image = jnp.concatenate(
        [
            jnp.concatenate(
                [x[:, lo + 32 * h : lo + 32 * h + 32] for h in range(2) for x in parts], axis=1
            )
            for lo in (0, 64)
        ],
        axis=0,
    )
    direction = rhs_ref[...]
    sol_ref[...] = step * direction
    res_ref[...] = direction - step * (scale * image + noise * direction)


def on_device(encodings, first_weight, second_weight, inv_scale, outputscale, noise, rhs):
    sent = pl.pallas_call(
        pack_kernel,
        out_shape=jax.ShapeDtypeStruct((PEERS, 32, 128), F32),
        scratch_shapes=[pltpu.VMEM((P_SETS, 16, 128), F32)],
        name="features",
    )(encodings, first_weight, second_weight, inv_scale.reshape(1, -1), rhs)
    own = lax.all_to_all(sent, ("xh", "g"), 0, 0, tiled=True)
    other = lax.ppermute(own[:, 16:], "c", [(0, 1), (1, 0)])
    rows, columns = CHIPS * 64, 2 * CHIPS * 64
    partial = pl.pallas_call(
        product_kernel,
        out_shape=jax.ShapeDtypeStruct((PEERS, 16, 128), F32),
        scratch_shapes=[
            pltpu.VMEM((rows, DEPTH), BF16),
            pltpu.VMEM((DEPTH, columns), BF16),
            pltpu.VMEM((columns, 64), BF16),
            pltpu.VMEM((CHIPS // 2, 32, 128), F32),
            pltpu.VMEM((rows, 64), F32),
        ],
        compiler_params=pltpu.CompilerParams(vmem_limit_bytes=32 << 20),
        name="kernel_product",
    )(own, other)
    got = lax.all_to_all(partial, ("xh", "g"), 0, 0, tiled=True)
    sums = jnp.sum(got[:, 8:], axis=0)
    far = lax.ppermute(sums, "c", [(0, 1), (1, 0)])
    vmem, smem = pl.BlockSpec(memory_space=pltpu.VMEM), pl.BlockSpec(memory_space=pltpu.SMEM)
    return pl.pallas_call(
        finish_kernel,
        out_shape=(jax.ShapeDtypeStruct(rhs.shape, F32),) * 2,
        in_specs=[vmem, vmem, vmem, vmem, smem, smem],
        name="update",
    )(got, sums, far, rhs, outputscale, noise)


def solution(mesh):
    split = Mesh(mesh.devices.reshape(CHIPS, 2, 2), ("g", "c", "xh"))
    vectors = P("xh", ("g", "c"))
    return jax.shard_map(
        on_device,
        mesh=split,
        in_specs=(P(("g", "c", "xh"), None), P(), P(), P(), P(), P(), vectors),
        out_specs=(vectors, vectors),
        check_vma=False,
    )
```

```python
import jax
import jax.numpy as jnp
from jax import lax
from jax.experimental import pallas as pl
from jax.experimental.pallas import tpu as pltpu
from jax.sharding import Mesh
from jax.sharding import PartitionSpec as P

F32, BF16 = jnp.float32, jnp.bfloat16
ROOT_LOG2E = 1.2011224087864498
CHIPS = 32
PEERS = 64
P_SETS = 8
WIDTH = 32
DEPTH = 256


def halves(x):
    high = x.astype(BF16)
    return high, (x - high.astype(F32)).astype(BF16)


def pack_kernel(enc_ref, w1_ref, w2_ref, inv_ref, rhs_ref, out_ref, set_ref):
    hidden = jnp.maximum(
        jnp.dot(enc_ref[...], w1_ref[...], preferred_element_type=F32), 0.0
    ).astype(BF16)
    features = lax.dot_general(
        w2_ref[...], hidden, (((1,), (1,)), ((), ())), preferred_element_type=F32
    )
    n = features.shape[0]
    diagonal = lax.broadcasted_iota(jnp.int32, (n, n), 0) == lax.broadcasted_iota(
        jnp.int32, (n, n), 1
    )
    inv = jnp.sum(
        jnp.where(diagonal, jnp.broadcast_to(inv_ref[...], (n, n)), 0.0), axis=1, keepdims=True
    )
    features = features * inv * ROOT_LOG2E
    half = rhs_ref.shape[1] // 2
    for p in range(P_SETS):
        at = slice(WIDTH * p, WIDTH * (p + 1))
        late = slice(half + WIDTH * p, half + WIDTH * (p + 1))
        set_ref[p] = jnp.concatenate(
            [features[:16, at], features[16:, at], rhs_ref[:, at], rhs_ref[:, late]], axis=1
        )
    for k in range(PEERS):
        out_ref[k, :16] = set_ref[k // P_SETS]
        out_ref[k, 16:] = set_ref[k % P_SETS]


def points_of(ref, k, lo):
    a0, a1 = ref[2 * k, lo : lo + 16], ref[2 * k + 1, lo : lo + 16]
    b0, b1 = ref[CHIPS + 2 * k, lo : lo + 16], ref[CHIPS + 2 * k + 1, lo : lo + 16]
    four = (a0, b0, a1, b1)
    features = jnp.concatenate(
        [
            jnp.concatenate([x[:, :32] for x in four], axis=1),
            jnp.concatenate([x[:, 32:64] for x in four], axis=1),
        ],
        axis=0,
    )
    columns = jnp.concatenate(
        [
            jnp.concatenate([a0[:, 64:], a1[:, 64:]], axis=1),
            jnp.concatenate([b0[:, 64:], b1[:, 64:]], axis=1),
        ],
        axis=0,
    )
    return features, columns


def operand(features, left):
    y1, y2 = halves(features)
    kept = y1.astype(F32) + y2.astype(F32)
    norm = -0.5 * jnp.sum(kept * kept, axis=0, keepdims=True)
    n1 = norm.astype(BF16).astype(F32)
    n2 = (norm - n1).astype(BF16).astype(F32)
    n3 = norm - n1 - n2
    row = lax.broadcasted_iota(jnp.int32, (16, features.shape[1]), 0)
    own, other = (3, 0) if left else (0, 3)
    tail = jnp.where(
        row == own,
        n1,
        jnp.where(
            row == own + 1,
            n2,
            jnp.where(
                row == own + 2, n3, jnp.where((row >= other) & (row < other + 3), 1.0, 0.0)
            ),
        ),
    ).astype(BF16)
    blank = jnp.zeros((DEPTH - 144, features.shape[1]), BF16)
    parts = [y1, y1, y2, y2] if left else [y1, y2, y1, y2]
    return jnp.concatenate(parts + [tail, blank], axis=0)


def product_kernel(own_ref, other_ref, out_ref, left_ref, right_ref, vec_ref, rows_ref, acc_ref):
    tiles = CHIPS // 2

    def prepare(k, _):
        features, columns = points_of(own_ref, k, 0)
        at = pl.ds(pl.multiple_of(k * 128, 128), 128)
        left_ref[at, :] = operand(features, True).T
        rows_ref[k] = columns
        for n, (ref, lo) in enumerate(((own_ref, 16), (other_ref, 0))):
            features, columns = points_of(ref, k, lo)
            at = pl.ds(pl.multiple_of((n * tiles + k) * 128, 128), 128)
            right_ref[:, at] = operand(features, False)
            v1, v2 = halves(columns)
            vec_ref[at, :] = jnp.concatenate([v1, v2], axis=0).T
        return 0

    lax.fori_loop(0, tiles, prepare, 0)
    acc_ref[...] = jnp.zeros_like(acc_ref)

    def multiply(j, _):
        at = pl.ds(pl.multiple_of(j * 256, 256), 256)
        right = right_ref[:, at]
        vec = vec_ref[at, :]
        for r in range(left_ref.shape[0] // 256):
            rows = slice(256 * r, 256 * (r + 1))
            exponent = jnp.dot(left_ref[rows, :], right, preferred_element_type=F32)
            tile = jnp.exp2(exponent).astype(BF16)
            acc_ref[rows, :] += jnp.dot(tile, vec, preferred_element_type=F32)
        return 0

    lax.fori_loop(0, right_ref.shape[1] // 256, multiply, 0)

    product = jnp.zeros((32, 128), F32)
    square = jnp.zeros((32, 128), F32)
    for k in range(tiles):
        both = acc_ref[128 * k : 128 * (k + 1), :].T
        image = both[:32] + both[32:]
        rows = rows_ref[k]
        product = product + rows * image
        square = square + rows * rows
        for xh in range(2):
            top, low = image[16 * xh : 16 * xh + 8], image[16 * xh + 8 : 16 * xh + 16]
            for chip in range(2):
                at = slice(64 * chip, 64 * (chip + 1))
                out_ref[CHIPS * xh + 2 * k + chip, :8] = jnp.concatenate(
                    [top[:, at], low[:, at]], axis=1
                )
    product = jnp.sum(product, axis=1, keepdims=True)
    square = jnp.sum(square, axis=1, keepdims=True) * (P_SETS / PEERS)
    lane = lax.broadcasted_iota(jnp.int32, (8, 128), 1)
    for xh in range(2):
        sums = jnp.zeros((8, 128), F32)
        for n, x in enumerate((product, square)):
            for a in range(2):
                lo = 16 * xh + 8 * a
                sums = jnp.where(lane == 2 * n + a, x[lo : lo + 8], sums)
        out_ref[CHIPS * xh : CHIPS * (xh + 1), 8:] = jnp.broadcast_to(sums, (CHIPS, 8, 128))


def finish_kernel(got_ref, own_ref, other_ref, rhs_ref, scale_ref, noise_ref, sol_ref, res_ref):
    scale, noise = scale_ref[0], noise_ref[0]
    sums = own_ref[...] + other_ref[...]
    product = jnp.concatenate([sums[:, 0:1], sums[:, 1:2]], axis=0)
    square = jnp.concatenate([sums[:, 2:3], sums[:, 3:4]], axis=0)
    step = square / (scale * product + noise * square)
    per = PEERS // P_SETS
    parts = []
    for p in range(P_SETS):
        part = got_ref[per * p, :8]
        for q in range(1, per):
            part = part + got_ref[per * p + q, :8]
        parts.append(part)
    image = jnp.concatenate(
        [
            jnp.concatenate(
                [x[:, lo + 32 * h : lo + 32 * h + 32] for h in range(2) for x in parts], axis=1
            )
            for lo in (0, 64)
        ],
        axis=0,
    )
    direction = rhs_ref[...]
    sol_ref[...] = step * direction
    res_ref[...] = direction - step * (scale * image + noise * direction)


def on_device(encodings, first_weight, second_weight, inv_scale, outputscale, noise, rhs):
    sent = pl.pallas_call(
        pack_kernel,
        out_shape=jax.ShapeDtypeStruct((PEERS, 32, 128), F32),
        scratch_shapes=[pltpu.VMEM((P_SETS, 16, 128), F32)],
        compiler_params=pltpu.CompilerParams(vmem_limit_bytes=8 << 20),
        name="features",
    )(encodings, first_weight, second_weight.T, inv_scale.reshape(1, -1), rhs)
    own = lax.all_to_all(sent, ("xh", "g"), 0, 0, tiled=True)
    other = lax.ppermute(own[:, 16:], "c", [(0, 1), (1, 0)])
    rows, columns = CHIPS * 64, 2 * CHIPS * 64
    partial = pl.pallas_call(
        product_kernel,
        out_shape=jax.ShapeDtypeStruct((PEERS, 16, 128), F32),
        scratch_shapes=[
            pltpu.VMEM((rows, DEPTH), BF16),
            pltpu.VMEM((DEPTH, columns), BF16),
            pltpu.VMEM((columns, 64), BF16),
            pltpu.VMEM((CHIPS // 2, 32, 128), F32),
            pltpu.VMEM((rows, 64), F32),
        ],
        compiler_params=pltpu.CompilerParams(vmem_limit_bytes=32 << 20),
        name="kernel_product",
    )(own, other)
    got = lax.all_to_all(partial, ("xh", "g"), 0, 0, tiled=True)
    sums = jnp.sum(got[:, 8:], axis=0)
    far = lax.ppermute(sums, "c", [(0, 1), (1, 0)])
    vmem, smem = pl.BlockSpec(memory_space=pltpu.VMEM), pl.BlockSpec(memory_space=pltpu.SMEM)
    return pl.pallas_call(
        finish_kernel,
        out_shape=(jax.ShapeDtypeStruct(rhs.shape, F32),) * 2,
        in_specs=[vmem, vmem, vmem, vmem, smem, smem],
        compiler_params=pltpu.CompilerParams(vmem_limit_bytes=8 << 20),
        name="update",
    )(got, sums, far, rhs, outputscale, noise)


def solution(mesh):
    split = Mesh(mesh.devices.reshape(CHIPS, 2, 2), ("g", "c", "xh"))
    vectors = P("xh", ("g", "c"))
    return jax.shard_map(
        on_device,
        mesh=split,
        in_specs=(P(("g", "c", "xh"), None), P(), P(), P(), P(), P(), vectors),
        out_specs=(vectors, vectors),
        check_vma=False,
    )
```

```python
import jax
import jax.numpy as jnp
from jax import lax
from jax.experimental import pallas as pl
from jax.experimental.pallas import tpu as pltpu
from jax.sharding import Mesh
from jax.sharding import PartitionSpec as P

F32, BF16 = jnp.float32, jnp.bfloat16
ROOT_LOG2E = 1.2011224087864498
CHIPS = 32
PEERS = 64
P_SETS = 8
WIDTH = 32
DEPTH = 256
STEPS = 4
STRIP = 2048
ROWS = 128


def halves(x):
    high = x.astype(BF16)
    return high, (x - high.astype(F32)).astype(BF16)


def pack_kernel(
    enc_hbm, w1_hbm, w2_hbm, inv_hbm, scale_hbm, noise_hbm, rhs_hbm,
    out_ref, pair_ref,
    enc_ref, w1_ref, w2_ref, inv_ref, scale_ref, noise_ref, rhs_ref, set_ref, big_sem, sem,
):
    small = [
        pltpu.make_async_copy(src, dst, sem.at[n])
        for n, (src, dst) in enumerate(
            (
                (w2_hbm, w2_ref),
                (inv_hbm, inv_ref),
                (rhs_hbm, rhs_ref),
                (scale_hbm, scale_ref),
                (noise_hbm, noise_ref),
            )
        )
    ]
    depth = enc_hbm.shape[1] // STEPS
    big = []
    for n in range(STEPS):
        at = pl.ds(n * depth, depth)
        big.append(
            (
                pltpu.make_async_copy(enc_hbm.at[:, at], enc_ref.at[:, at], big_sem.at[2 * n]),
                pltpu.make_async_copy(w1_hbm.at[at], w1_ref.at[at], big_sem.at[2 * n + 1]),
            )
        )
    for pair in big:
        for copy in pair:
            copy.start()
    for copy in small:
        copy.start()
    hidden = jnp.zeros((enc_hbm.shape[0], w1_hbm.shape[1]), F32)
    for n in range(STEPS):
        at = slice(n * depth, (n + 1) * depth)
        for copy in big[n]:
            copy.wait()
        hidden = hidden + jnp.dot(enc_ref[:, at], w1_ref[at], preferred_element_type=F32)
    hidden = jnp.maximum(hidden, 0.0).astype(BF16)
    for copy in small:
        copy.wait()
    pair_ref[:4] = jnp.broadcast_to(scale_ref[...], (4, 128))
    pair_ref[4:] = jnp.broadcast_to(noise_ref[...], (4, 128))
    features = lax.dot_general(
        w2_ref[...], hidden, (((1,), (1,)), ((), ())), preferred_element_type=F32
    )
    n = features.shape[0]
    diagonal = lax.broadcasted_iota(jnp.int32, (n, n), 0) == lax.broadcasted_iota(
        jnp.int32, (n, n), 1
    )
    inv = jnp.sum(
        jnp.where(diagonal, jnp.broadcast_to(inv_ref[...], (n, n)), 0.0), axis=1, keepdims=True
    )
    features = features * inv * ROOT_LOG2E
    half = rhs_ref.shape[1] // 2
    for p in range(P_SETS):
        at = slice(WIDTH * p, WIDTH * (p + 1))
        late = slice(half + WIDTH * p, half + WIDTH * (p + 1))
        set_ref[p] = jnp.concatenate(
            [features[:16, at], features[16:, at], rhs_ref[:, at], rhs_ref[:, late]], axis=1
        )
    for k in range(PEERS):
        out_ref[k, :16] = set_ref[k // P_SETS]
        out_ref[k, 16:] = set_ref[k % P_SETS]


def points_of(ref, k, lo):
    a0, a1 = ref[2 * k, lo : lo + 16], ref[2 * k + 1, lo : lo + 16]
    b0, b1 = ref[CHIPS + 2 * k, lo : lo + 16], ref[CHIPS + 2 * k + 1, lo : lo + 16]
    four = (a0, b0, a1, b1)
    features = jnp.concatenate(
        [
            jnp.concatenate([x[:, :32] for x in four], axis=1),
            jnp.concatenate([x[:, 32:64] for x in four], axis=1),
        ],
        axis=0,
    )
    columns = jnp.concatenate(
        [
            jnp.concatenate([a0[:, 64:], a1[:, 64:]], axis=1),
            jnp.concatenate([b0[:, 64:], b1[:, 64:]], axis=1),
        ],
        axis=0,
    )
    return features, columns


def operand(features, left):
    y1, y2 = halves(features)
    kept = y1.astype(F32) + y2.astype(F32)
    norm = -0.5 * jnp.sum(kept * kept, axis=0, keepdims=True)
    n1 = norm.astype(BF16).astype(F32)
    n2 = (norm - n1).astype(BF16).astype(F32)
    n3 = norm - n1 - n2
    row = lax.broadcasted_iota(jnp.int32, (16, features.shape[1]), 0)
    own, other = (3, 0) if left else (0, 3)
    tail = jnp.where(
        row == own,
        n1,
        jnp.where(
            row == own + 1,
            n2,
            jnp.where(
                row == own + 2, n3, jnp.where((row >= other) & (row < other + 3), 1.0, 0.0)
            ),
        ),
    ).astype(BF16)
    blank = jnp.zeros((DEPTH - 144, features.shape[1]), BF16)
    parts = [y1, y1, y2, y2] if left else [y1, y2, y1, y2]
    return jnp.concatenate(parts + [tail, blank], axis=0)


def product_kernel(own_ref, other_ref, out_ref, left_ref, right_ref, vec_ref, rows_ref):
    tiles = CHIPS // 2

    for k in range(tiles):
        features, columns = points_of(own_ref, k, 0)
        at = slice(k * 128, (k + 1) * 128)
        left_ref[at, :] = operand(features, True).T
        rows_ref[k] = columns
        for n, (ref, lo) in enumerate(((own_ref, 16), (other_ref, 0))):
            features, columns = points_of(ref, k, lo)
            at = slice((n * tiles + k) * 128, (n * tiles + k + 1) * 128)
            right_ref[:, at] = operand(features, False)
            v1, v2 = halves(columns)
            vec_ref[at, :] = jnp.concatenate([v1, v2], axis=0).T
    product = jnp.zeros((32, 128), F32)
    square = jnp.zeros((32, 128), F32)
    for r in range(left_ref.shape[0] // ROWS):
        left = left_ref[ROWS * r : ROWS * (r + 1), :]
        total = jnp.zeros((ROWS, 64), F32)
        for j in range(right_ref.shape[1] // STRIP):
            at = slice(STRIP * j, STRIP * (j + 1))
            exponent = jnp.dot(left, right_ref[:, at], preferred_element_type=F32)
            tile = jnp.exp2(exponent).astype(BF16)
            total = total + jnp.dot(tile, vec_ref[at, :], preferred_element_type=F32)
        for k in range(ROWS // 128 * r, ROWS // 128 * (r + 1)):
            lo = 128 * k - ROWS * r
            both = total[lo : lo + 128].T
            image = both[:32] + both[32:]
            rows = rows_ref[k]
            product = product + rows * image
            square = square + rows * rows
            for xh in range(2):
                top, low = image[16 * xh : 16 * xh + 8], image[16 * xh + 8 : 16 * xh + 16]
                for chip in range(2):
                    at = slice(64 * chip, 64 * (chip + 1))
                    out_ref[CHIPS * xh + 2 * k + chip, :8] = jnp.concatenate(
                        [top[:, at], low[:, at]], axis=1
                    )
    product = jnp.sum(product, axis=1, keepdims=True)
    square = jnp.sum(square, axis=1, keepdims=True) * (P_SETS / PEERS)
    lane = lax.broadcasted_iota(jnp.int32, (8, 128), 1)
    for xh in range(2):
        sums = jnp.zeros((8, 128), F32)
        for n, x in enumerate((product, square)):
            for a in range(2):
                lo = 16 * xh + 8 * a
                sums = jnp.where(lane == 2 * n + a, x[lo : lo + 8], sums)
        out_ref[CHIPS * xh : CHIPS * (xh + 1), 8:] = jnp.broadcast_to(sums, (CHIPS, 8, 128))


def finish_kernel(got_ref, own_ref, other_ref, rhs_ref, pair_ref, sol_ref, res_ref):
    scale, noise = pair_ref[0:1, 0:1], pair_ref[4:5, 0:1]
    sums = own_ref[...] + other_ref[...]
    product = jnp.concatenate([sums[:, 0:1], sums[:, 1:2]], axis=0)
    square = jnp.concatenate([sums[:, 2:3], sums[:, 3:4]], axis=0)
    step = square / (scale * product + noise * square)
    per = PEERS // P_SETS
    parts = []
    for p in range(P_SETS):
        part = got_ref[per * p, :8]
        for q in range(1, per):
            part = part + got_ref[per * p + q, :8]
        parts.append(part)
    image = jnp.concatenate(
        [
            jnp.concatenate(
                [x[:, lo + 32 * h : lo + 32 * h + 32] for h in range(2) for x in parts], axis=1
            )
            for lo in (0, 64)
        ],
        axis=0,
    )
    direction = rhs_ref[...]
    sol_ref[...] = step * direction
    res_ref[...] = direction - step * (scale * image + noise * direction)


def on_device(encodings, first_weight, second_weight, inv_scale, outputscale, noise, rhs):
    hbm, vmem = pl.BlockSpec(memory_space=pltpu.HBM), pl.BlockSpec(memory_space=pltpu.VMEM)
    sent, pair = pl.pallas_call(
        pack_kernel,
        out_shape=(
            jax.ShapeDtypeStruct((PEERS, 32, 128), F32),
            jax.ShapeDtypeStruct((8, 128), F32),
        ),
        in_specs=[hbm] * 7,
        scratch_shapes=[
            pltpu.VMEM(encodings.shape, BF16),
            pltpu.VMEM(first_weight.shape, BF16),
            pltpu.VMEM(second_weight.shape[::-1], BF16),
            pltpu.VMEM((1, inv_scale.size), F32),
            pltpu.VMEM((1, 1), F32),
            pltpu.VMEM((1, 1), F32),
            pltpu.VMEM(rhs.shape, F32),
            pltpu.VMEM((P_SETS, 16, 128), F32),
            pltpu.SemaphoreType.DMA((2 * STEPS,)),
            pltpu.SemaphoreType.DMA((5,)),
        ],
        name="features",
    )(
        encodings,
        first_weight,
        second_weight.T,
        inv_scale.reshape(1, -1),
        outputscale.reshape(1, 1),
        noise.reshape(1, 1),
        rhs,
    )
    own = lax.all_to_all(sent, ("xh", "g"), 0, 0, tiled=True)
    other = lax.ppermute(own[:, 16:], "c", [(0, 1), (1, 0)])
    rows, columns = CHIPS * 64, 2 * CHIPS * 64
    partial = pl.pallas_call(
        product_kernel,
        out_shape=jax.ShapeDtypeStruct((PEERS, 16, 128), F32),
        scratch_shapes=[
            pltpu.VMEM((rows, DEPTH), BF16),
            pltpu.VMEM((DEPTH, columns), BF16),
            pltpu.VMEM((columns, 64), BF16),
            pltpu.VMEM((CHIPS // 2, 32, 128), F32),
        ],
        compiler_params=pltpu.CompilerParams(vmem_limit_bytes=32 << 20),
        name="kernel_product",
    )(own, other)
    got = lax.all_to_all(partial, ("xh", "g"), 0, 0, tiled=True)
    sums = jnp.sum(got[:, 8:], axis=0)
    far = lax.ppermute(sums, "c", [(0, 1), (1, 0)])
    return pl.pallas_call(
        finish_kernel,
        out_shape=(jax.ShapeDtypeStruct(rhs.shape, F32),) * 2,
        in_specs=[vmem] * 5,
        compiler_params=pltpu.CompilerParams(vmem_limit_bytes=8 << 20),
        name="update",
    )(got, sums, far, rhs, pair)


def solution(mesh):
    split = Mesh(mesh.devices.reshape(CHIPS, 2, 2), ("g", "c", "xh"))
    vectors = P("xh", ("g", "c"))
    return jax.shard_map(
        on_device,
        mesh=split,
        in_specs=(P(("g", "c", "xh"), None), P(), P(), P(), P(), P(), vectors),
        out_specs=(vectors, vectors),
        check_vma=False,
    )
```

```python
import jax
import jax.numpy as jnp
from jax import lax
from jax.experimental import pallas as pl
from jax.experimental.pallas import tpu as pltpu
from jax.sharding import Mesh
from jax.sharding import PartitionSpec as P

F32, BF16 = jnp.float32, jnp.bfloat16
ROOT_LOG2E = 1.2011224087864498
CHIPS = 32
PEERS = 64
P_SETS = 8
WIDTH = 32
DEPTH = 256
STEPS = 4
STRIP = 2048
ROWS = 128


def halves(x):
    high = x.astype(BF16)
    return high, (x - high.astype(F32)).astype(BF16)


def pack_kernel(
    enc_hbm, w1_hbm, w2_hbm, inv_hbm, rhs_hbm, out_ref,
    enc_ref, w1_ref, w2_ref, inv_ref, rhs_ref, set_ref, big_sem, sem,
):
    small = [
        pltpu.make_async_copy(src, dst, sem.at[n])
        for n, (src, dst) in enumerate(
            (
                (w2_hbm, w2_ref),
                (inv_hbm, inv_ref),
                (rhs_hbm, rhs_ref),
            )
        )
    ]
    depth = enc_hbm.shape[1] // STEPS
    big = []
    for n in range(STEPS):
        at = pl.ds(n * depth, depth)
        big.append(
            (
                pltpu.make_async_copy(enc_hbm.at[:, at], enc_ref.at[:, at], big_sem.at[2 * n]),
                pltpu.make_async_copy(w1_hbm.at[at], w1_ref.at[at], big_sem.at[2 * n + 1]),
            )
        )
    for pair in big:
        for copy in pair:
            copy.start()
    for copy in small:
        copy.start()
    hidden = jnp.zeros((enc_hbm.shape[0], w1_hbm.shape[1]), F32)
    for n in range(STEPS):
        at = slice(n * depth, (n + 1) * depth)
        for copy in big[n]:
            copy.wait()
        hidden = hidden + jnp.dot(enc_ref[:, at], w1_ref[at], preferred_element_type=F32)
    hidden = jnp.maximum(hidden, 0.0).astype(BF16)
    for copy in small:
        copy.wait()
    features = lax.dot_general(
        w2_ref[...], hidden, (((1,), (1,)), ((), ())), preferred_element_type=F32
    )
    n = features.shape[0]
    diagonal = lax.broadcasted_iota(jnp.int32, (n, n), 0) == lax.broadcasted_iota(
        jnp.int32, (n, n), 1
    )
    inv = jnp.sum(
        jnp.where(diagonal, jnp.broadcast_to(inv_ref[...], (n, n)), 0.0), axis=1, keepdims=True
    )
    features = features * inv * ROOT_LOG2E
    half = rhs_ref.shape[1] // 2
    for p in range(P_SETS):
        at = slice(WIDTH * p, WIDTH * (p + 1))
        late = slice(half + WIDTH * p, half + WIDTH * (p + 1))
        set_ref[p] = jnp.concatenate(
            [features[:16, at], features[16:, at], rhs_ref[:, at], rhs_ref[:, late]], axis=1
        )
    for k in range(PEERS):
        out_ref[k, :16] = set_ref[k // P_SETS]
        out_ref[k, 16:] = set_ref[k % P_SETS]


def points_of(ref, k, lo):
    a0, a1 = ref[2 * k, lo : lo + 16], ref[2 * k + 1, lo : lo + 16]
    b0, b1 = ref[CHIPS + 2 * k, lo : lo + 16], ref[CHIPS + 2 * k + 1, lo : lo + 16]
    four = (a0, b0, a1, b1)
    features = jnp.concatenate(
        [
            jnp.concatenate([x[:, :32] for x in four], axis=1),
            jnp.concatenate([x[:, 32:64] for x in four], axis=1),
        ],
        axis=0,
    )
    columns = jnp.concatenate(
        [
            jnp.concatenate([a0[:, 64:], a1[:, 64:]], axis=1),
            jnp.concatenate([b0[:, 64:], b1[:, 64:]], axis=1),
        ],
        axis=0,
    )
    return features, columns


def operand(features, left):
    y1, y2 = halves(features)
    kept = y1.astype(F32) + y2.astype(F32)
    norm = -0.5 * jnp.sum(kept * kept, axis=0, keepdims=True)
    n1 = norm.astype(BF16).astype(F32)
    n2 = (norm - n1).astype(BF16).astype(F32)
    n3 = norm - n1 - n2
    row = lax.broadcasted_iota(jnp.int32, (16, features.shape[1]), 0)
    own, other = (3, 0) if left else (0, 3)
    tail = jnp.where(
        row == own,
        n1,
        jnp.where(
            row == own + 1,
            n2,
            jnp.where(
                row == own + 2, n3, jnp.where((row >= other) & (row < other + 3), 1.0, 0.0)
            ),
        ),
    ).astype(BF16)
    blank = jnp.zeros((DEPTH - 144, features.shape[1]), BF16)
    parts = [y1, y1, y2, y2] if left else [y1, y2, y1, y2]
    return jnp.concatenate(parts + [tail, blank], axis=0)


def product_kernel(own_ref, other_ref, out_ref, left_ref, right_ref, vec_ref, rows_ref):
    tiles = CHIPS // 2

    for k in range(tiles):
        features, columns = points_of(own_ref, k, 0)
        at = slice(k * 128, (k + 1) * 128)
        left_ref[at, :] = operand(features, True).T
        rows_ref[k] = columns
        for n, (ref, lo) in enumerate(((own_ref, 16), (other_ref, 0))):
            features, columns = points_of(ref, k, lo)
            at = slice((n * tiles + k) * 128, (n * tiles + k + 1) * 128)
            right_ref[:, at] = operand(features, False)
            v1, v2 = halves(columns)
            vec_ref[at, :] = jnp.concatenate([v1, v2], axis=0).T
    product = jnp.zeros((32, 128), F32)
    square = jnp.zeros((32, 128), F32)
    for r in range(left_ref.shape[0] // ROWS):
        left = left_ref[ROWS * r : ROWS * (r + 1), :]
        total = jnp.zeros((ROWS, 64), F32)
        for j in range(right_ref.shape[1] // STRIP):
            at = slice(STRIP * j, STRIP * (j + 1))
            exponent = jnp.dot(left, right_ref[:, at], preferred_element_type=F32)
            tile = jnp.exp2(exponent).astype(BF16)
            total = total + jnp.dot(tile, vec_ref[at, :], preferred_element_type=F32)
        for k in range(ROWS // 128 * r, ROWS // 128 * (r + 1)):
            lo = 128 * k - ROWS * r
            both = total[lo : lo + 128].T
            image = both[:32] + both[32:]
            rows = rows_ref[k]
            product = product + rows * image
            square = square + rows * rows
            for xh in range(2):
                top, low = image[16 * xh : 16 * xh + 8], image[16 * xh + 8 : 16 * xh + 16]
                for chip in range(2):
                    at = slice(64 * chip, 64 * (chip + 1))
                    out_ref[CHIPS * xh + 2 * k + chip, :8] = jnp.concatenate(
                        [top[:, at], low[:, at]], axis=1
                    )
    product = jnp.sum(product, axis=1, keepdims=True)
    square = jnp.sum(square, axis=1, keepdims=True) * (P_SETS / PEERS)
    lane = lax.broadcasted_iota(jnp.int32, (8, 128), 1)
    for xh in range(2):
        sums = jnp.zeros((8, 128), F32)
        for n, x in enumerate((product, square)):
            for a in range(2):
                lo = 16 * xh + 8 * a
                sums = jnp.where(lane == 2 * n + a, x[lo : lo + 8], sums)
        out_ref[CHIPS * xh : CHIPS * (xh + 1), 8:] = jnp.broadcast_to(sums, (CHIPS, 8, 128))


def finish_kernel(got_ref, own_ref, other_ref, rhs_ref, scale_ref, noise_ref, sol_ref, res_ref):
    scale, noise = scale_ref[...], noise_ref[...]
    sums = own_ref[...] + other_ref[...]
    product = jnp.concatenate([sums[:, 0:1], sums[:, 1:2]], axis=0)
    square = jnp.concatenate([sums[:, 2:3], sums[:, 3:4]], axis=0)
    step = square / (scale * product + noise * square)
    per = PEERS // P_SETS
    parts = []
    for p in range(P_SETS):
        part = got_ref[per * p, :8]
        for q in range(1, per):
            part = part + got_ref[per * p + q, :8]
        parts.append(part)
    image = jnp.concatenate(
        [
            jnp.concatenate(
                [x[:, lo + 32 * h : lo + 32 * h + 32] for h in range(2) for x in parts], axis=1
            )
            for lo in (0, 64)
        ],
        axis=0,
    )
    direction = rhs_ref[...]
    sol_ref[...] = step * direction
    res_ref[...] = direction - step * (scale * image + noise * direction)


def on_device(encodings, first_weight, second_weight, inv_scale, outputscale, noise, rhs):
    hbm, vmem = pl.BlockSpec(memory_space=pltpu.HBM), pl.BlockSpec(memory_space=pltpu.VMEM)
    sent = pl.pallas_call(
        pack_kernel,
        out_shape=jax.ShapeDtypeStruct((PEERS, 32, 128), F32),
        in_specs=[hbm] * 5,
        scratch_shapes=[
            pltpu.VMEM(encodings.shape, BF16),
            pltpu.VMEM(first_weight.shape, BF16),
            pltpu.VMEM(second_weight.shape[::-1], BF16),
            pltpu.VMEM((1, inv_scale.size), F32),
            pltpu.VMEM(rhs.shape, F32),
            pltpu.VMEM((P_SETS, 16, 128), F32),
            pltpu.SemaphoreType.DMA((2 * STEPS,)),
            pltpu.SemaphoreType.DMA((3,)),
        ],
        name="features",
    )(
        encodings,
        first_weight,
        second_weight.T,
        inv_scale.reshape(1, -1),
        rhs,
    )
    own = lax.all_to_all(sent, ("xh", "g"), 0, 0, tiled=True)
    other = lax.ppermute(own[:, 16:], "c", [(0, 1), (1, 0)])
    rows, columns = CHIPS * 64, 2 * CHIPS * 64
    partial = pl.pallas_call(
        product_kernel,
        out_shape=jax.ShapeDtypeStruct((PEERS, 16, 128), F32),
        scratch_shapes=[
            pltpu.VMEM((rows, DEPTH), BF16),
            pltpu.VMEM((DEPTH, columns), BF16),
            pltpu.VMEM((columns, 64), BF16),
            pltpu.VMEM((CHIPS // 2, 32, 128), F32),
        ],
        compiler_params=pltpu.CompilerParams(vmem_limit_bytes=32 << 20),
        name="kernel_product",
    )(own, other)
    got = lax.all_to_all(partial, ("xh", "g"), 0, 0, tiled=True)
    sums = jnp.sum(got[:, 8:], axis=0)
    far = lax.ppermute(sums, "c", [(0, 1), (1, 0)])
    return pl.pallas_call(
        finish_kernel,
        out_shape=(jax.ShapeDtypeStruct(rhs.shape, F32),) * 2,
        in_specs=[vmem] * 6,
        compiler_params=pltpu.CompilerParams(vmem_limit_bytes=8 << 20),
        name="update",
    )(got, sums, far, rhs, outputscale.reshape(1, 1), noise.reshape(1, 1))


def solution(mesh):
    split = Mesh(mesh.devices.reshape(CHIPS, 2, 2), ("g", "c", "xh"))
    vectors = P("xh", ("g", "c"))
    return jax.shard_map(
        on_device,
        mesh=split,
        in_specs=(P(("g", "c", "xh"), None), P(), P(), P(), P(), P(), vectors),
        out_specs=(vectors, vectors),
        check_vma=False,
    )
```

```python
import jax
import jax.numpy as jnp
from jax import lax
from jax.experimental import pallas as pl
from jax.experimental.pallas import tpu as pltpu
from jax.sharding import Mesh
from jax.sharding import PartitionSpec as P

F32, BF16 = jnp.float32, jnp.bfloat16
ROOT_LOG2E = 1.2011224087864498
CHIPS = 32
PEERS = 64
GROUPS = 8
WIDTH = 32
DEPTH = 256
STEPS = 4
ROWS = 256
PAIRS = [(a, b, t) for a in range(GROUPS) for b in range(a + 1, GROUPS) for t in range(2)]
TILES = CHIPS // 2
HALF = TILES * 128 // 2


def halves(x):
    high = x.astype(BF16)
    return high, (x - high.astype(F32)).astype(BF16)


def pack_kernel(
    enc_hbm, w1_hbm, w2_hbm, inv_hbm, rhs_hbm, out_ref,
    enc_ref, w1_ref, w2_ref, inv_ref, rhs_ref, set_ref, part_ref, big_sem, sem,
):
    small = [
        pltpu.make_async_copy(src, dst, sem.at[n])
        for n, (src, dst) in enumerate(
            ((w2_hbm, w2_ref), (inv_hbm, inv_ref), (rhs_hbm, rhs_ref))
        )
    ]
    depth = enc_hbm.shape[1] // STEPS
    big = []
    for n in range(STEPS):
        at = pl.ds(n * depth, depth)
        big.append(
            (
                pltpu.make_async_copy(enc_hbm.at[:, at], enc_ref.at[:, at], big_sem.at[2 * n]),
                pltpu.make_async_copy(w1_hbm.at[at], w1_ref.at[at], big_sem.at[2 * n + 1]),
            )
        )
    for pair in big:
        for copy in pair:
            copy.start()
    for copy in small:
        copy.start()
    hidden = jnp.zeros((enc_hbm.shape[0], w1_hbm.shape[1]), F32)
    for n in range(STEPS):
        at = slice(n * depth, (n + 1) * depth)
        for copy in big[n]:
            copy.wait()
        hidden = hidden + jnp.dot(enc_ref[:, at], w1_ref[at], preferred_element_type=F32)
    hidden = jnp.maximum(hidden, 0.0).astype(BF16)
    for copy in small:
        copy.wait()
    features = lax.dot_general(
        w2_ref[...], hidden, (((1,), (1,)), ((), ())), preferred_element_type=F32
    )
    n = features.shape[0]
    diagonal = lax.broadcasted_iota(jnp.int32, (n, n), 0) == lax.broadcasted_iota(
        jnp.int32, (n, n), 1
    )
    inv = jnp.sum(
        jnp.where(diagonal, jnp.broadcast_to(inv_ref[...], (n, n)), 0.0), axis=1, keepdims=True
    )
    features = features * inv * ROOT_LOG2E
    late = rhs_ref.shape[1] // 2
    for a in range(GROUPS):
        lo = WIDTH * a
        at, after = slice(lo, lo + WIDTH), slice(late + lo, late + lo + WIDTH)
        set_ref[a] = jnp.concatenate(
            [features[:16, at], features[16:, at], rhs_ref[:, at], rhs_ref[:, after]], axis=1
        )
        for t in range(2):
            lo = WIDTH * a + 16 * t
            at, after = slice(lo, lo + 16), slice(late + lo, late + lo + 16)
            part_ref[2 * a + t] = jnp.concatenate(
                [features[8 * m : 8 * m + 8, at] for m in range(4)]
                + [rhs_ref[8 * m : 8 * m + 8, s] for m in range(2) for s in (at, after)],
                axis=1,
            )
    for k, (a, b, t) in enumerate(PAIRS):
        out_ref[k, :16] = set_ref[a]
        out_ref[k, 16:] = part_ref[2 * b + t]
    for a in range(GROUPS):
        out_ref[len(PAIRS) + a, :8] = jnp.zeros((8, 128), F32)
        out_ref[len(PAIRS) + a, 8:] = set_ref[a]


def points_of(ref, k, lo):
    a0, a1 = ref[2 * k, lo : lo + 16], ref[2 * k + 1, lo : lo + 16]
    b0, b1 = ref[CHIPS + 2 * k, lo : lo + 16], ref[CHIPS + 2 * k + 1, lo : lo + 16]
    four = (a0, b0, a1, b1)
    features = jnp.concatenate(
        [
            jnp.concatenate([x[:, :32] for x in four], axis=1),
            jnp.concatenate([x[:, 32:64] for x in four], axis=1),
        ],
        axis=0,
    )
    columns = jnp.concatenate(
        [
            jnp.concatenate([a0[:, 64:], a1[:, 64:]], axis=1),
            jnp.concatenate([b0[:, 64:], b1[:, 64:]], axis=1),
        ],
        axis=0,
    )
    return features, columns


def half_points_of(ref, k, lo):
    units = [[ref[CHIPS * xh + 4 * k + j, lo : lo + 8] for xh in range(2)] for j in range(4)]
    features = jnp.concatenate(
        [
            jnp.concatenate([u[:, 16 * m : 16 * m + 16] for pair in units for u in pair], axis=1)
            for m in range(4)
        ],
        axis=0,
    )
    columns = jnp.concatenate(
        [
            jnp.concatenate([pair[xh][:, s : s + 32] for pair in units], axis=1)
            for xh in range(2)
            for s in (64, 96)
        ],
        axis=0,
    )
    return features, columns


def operand(features, left):
    y1, y2 = halves(features)
    kept = y1.astype(F32) + y2.astype(F32)
    norm = -0.5 * jnp.sum(kept * kept, axis=0, keepdims=True)
    n1 = norm.astype(BF16).astype(F32)
    n2 = (norm - n1).astype(BF16).astype(F32)
    n3 = norm - n1 - n2
    row = lax.broadcasted_iota(jnp.int32, (16, features.shape[1]), 0)
    own, other = (3, 0) if left else (0, 3)
    tail = jnp.where(
        row == own,
        n1,
        jnp.where(
            row == own + 1,
            n2,
            jnp.where(
                row == own + 2, n3, jnp.where((row >= other) & (row < other + 3), 1.0, 0.0)
            ),
        ),
    ).astype(BF16)
    blank = jnp.zeros((DEPTH - 144, features.shape[1]), BF16)
    parts = [y1, y1, y2, y2] if left else [y1, y2, y1, y2]
    return jnp.concatenate(parts + [tail, blank], axis=0)


def product_kernel(
    own_ref, other_ref, out_ref, low_ref, far_ref,
    left_ref, right_ref, vec_ref, rows_ref, flat_ref, col_ref,
):
    on_pair = lax.axis_index("xh") * CHIPS + lax.axis_index("g") < len(PAIRS)
    lane = lax.broadcasted_iota(jnp.int32, (8, 128), 1)

    def set_rows(lo, flat):
        for k in range(TILES):
            features, columns = points_of(own_ref, k, lo)
            at = slice(k * 128, (k + 1) * 128)
            left_ref[at, :] = operand(features, True).T
            rows_ref[k] = columns
            if flat:
                flat_ref[:, at] = jnp.concatenate(halves(columns), axis=0)

    def set_columns(n, points):
        features, columns = points
        at = slice(n * 128, (n + 1) * 128)
        right_ref[:, at] = operand(features, False)
        vec_ref[at, :] = jnp.concatenate(halves(columns), axis=0).T

    def multiply(width, both_ways):
        product = jnp.zeros((32, 128), F32)
        square = jnp.zeros((32, 128), F32)
        for r in range(left_ref.shape[0] // ROWS):
            strip = slice(ROWS * r, ROWS * (r + 1))
            exponent = jnp.dot(
                left_ref[strip, :], right_ref[:, :width], preferred_element_type=F32
            )
            tile = jnp.exp2(exponent).astype(BF16)
            total = jnp.dot(tile, vec_ref[:width, :], preferred_element_type=F32)
            if both_ways:
                back = jnp.dot(flat_ref[:, strip], tile, preferred_element_type=F32)
                col_ref[...] = back if r == 0 else col_ref[...] + back
            for k in range(ROWS // 128 * r, ROWS // 128 * (r + 1)):
                lo = 128 * k - ROWS * r
                pair = total[lo : lo + 128].T
                image = pair[:32] + pair[32:]
                rows = rows_ref[k]
                product = product + rows * image
                if not both_ways:
                    square = square + rows * rows
                for xh in range(2):
                    top, low = image[16 * xh : 16 * xh + 8], image[16 * xh + 8 : 16 * xh + 16]
                    for chip in range(2):
                        at = slice(64 * chip, 64 * (chip + 1))
                        out_ref[CHIPS * xh + 2 * k + chip] = jnp.concatenate(
                            [top[:, at], low[:, at]], axis=1
                        )
        product = jnp.sum(product, axis=1, keepdims=True) * (2.0 if both_ways else 1.0)
        square = jnp.sum(square, axis=1, keepdims=True)
        sums = []
        for xh in range(2):
            here = jnp.zeros((8, 128), F32)
            for n, x in enumerate((product, square)):
                for a in range(2):
                    lo = 16 * xh + 8 * a
                    here = jnp.where(lane == 64 + 2 * n + a, x[lo : lo + 8], here)
            sums.append(here)
        return sums

    @pl.when(on_pair)
    def _():
        set_rows(0, True)
        for n in range(TILES // 2):
            set_columns(n, half_points_of(own_ref, n, 16))
        for n in range(TILES // 2):
            set_columns(TILES // 2 + n, half_points_of(other_ref, n, 8))
        sums = multiply(2 * HALF, True)
        for n in range(TILES):
            at = slice(n * 128, (n + 1) * 128)
            image = col_ref[:32, at] + col_ref[32:, at]
            k = n % (TILES // 2)
            for xh in range(2):
                for j in range(4):
                    at = slice(32 * j, 32 * j + 32)
                    part = jnp.concatenate(
                        [image[16 * xh : 16 * xh + 8, at], image[16 * xh + 8 : 16 * xh + 16, at]]
                        + [sums[xh][:, 64:]],
                        axis=1,
                    )
                    if n < TILES // 2:
                        low_ref[CHIPS * xh + 4 * k + j] = part
                    else:
                        far_ref[CHIPS * xh + 4 * k + j] = part

    @pl.when(jnp.logical_not(on_pair))
    def _():
        set_rows(8, False)
        for n in range(TILES):
            set_columns(n, points_of(own_ref, n, 8))
        for n in range(TILES):
            set_columns(TILES + n, points_of(other_ref, n, 0))
        sums = multiply(4 * HALF, False)
        for xh in range(2):
            at = slice(CHIPS * xh, CHIPS * (xh + 1))
            low_ref[at] = jnp.broadcast_to(sums[xh], (CHIPS, 8, 128))
            far_ref[at] = jnp.broadcast_to(sums[xh], (CHIPS, 8, 128))


def join_kernel(whole_ref, low_ref, near_ref, out_ref):
    out_ref[:, :8] = whole_ref[...]
    out_ref[:, 8:] = low_ref[...] + near_ref[...]


def finish_kernel(got_ref, rhs_ref, pair_ref, sol_ref, res_ref):
    scale, noise = pair_ref[0:1, 0:1], pair_ref[4:5, 0:1]
    whole = [None] * GROUPS
    part = [None] * (2 * GROUPS)
    sums = got_ref[len(PAIRS), 8:]

    def plus(x, y):
        return y if x is None else x + y

    for k, (a, b, t) in enumerate(PAIRS):
        low = got_ref[k, 8:]
        whole[a] = plus(whole[a], got_ref[k, :8])
        part[2 * b + t] = plus(part[2 * b + t], low)
        sums = sums + low
    for a in range(GROUPS):
        whole[a] = plus(whole[a], got_ref[len(PAIRS) + a, :8])
        if a:
            sums = sums + got_ref[len(PAIRS) + a, 8:]
    product = jnp.concatenate([sums[:, 64:65], sums[:, 65:66]], axis=0)
    square = jnp.concatenate([sums[:, 66:67], sums[:, 67:68]], axis=0)
    step = square / (scale * product + noise * square)
    image = jnp.concatenate(
        [
            jnp.concatenate(
                [
                    x[:, 64 * m + 32 * h : 64 * m + 32 * h + 32]
                    for h in range(2)
                    for x in whole
                ],
                axis=1,
            )
            for m in range(2)
        ],
        axis=0,
    )
    blank = jnp.zeros((8, 16), F32)
    image = image + jnp.concatenate(
        [
            jnp.concatenate(
                [
                    blank if x is None else x[:, 32 * m + 16 * h : 32 * m + 16 * h + 16]
                    for h in range(2)
                    for x in part
                ],
                axis=1,
            )
            for m in range(2)
        ],
        axis=0,
    )
    direction = rhs_ref[...]
    sol_ref[...] = step * direction
    res_ref[...] = direction - step * (scale * image + noise * direction)


def on_device(encodings, first_weight, second_weight, inv_scale, outputscale, noise, rhs):
    hbm, vmem = pl.BlockSpec(memory_space=pltpu.HBM), pl.BlockSpec(memory_space=pltpu.VMEM)
    swap = [(0, 1), (1, 0)]
    sent = pl.pallas_call(
        pack_kernel,
        out_shape=jax.ShapeDtypeStruct((PEERS, 24, 128), F32),
        in_specs=[hbm] * 5,
        scratch_shapes=[
            pltpu.VMEM(encodings.shape, BF16),
            pltpu.VMEM(first_weight.shape, BF16),
            pltpu.VMEM(second_weight.shape[::-1], BF16),
            pltpu.VMEM((1, inv_scale.size), F32),
            pltpu.VMEM(rhs.shape, F32),
            pltpu.VMEM((GROUPS, 16, 128), F32),
            pltpu.VMEM((2 * GROUPS, 8, 128), F32),
            pltpu.SemaphoreType.DMA((2 * STEPS,)),
            pltpu.SemaphoreType.DMA((3,)),
        ],
        name="features",
    )(encodings, first_weight, second_weight.T, inv_scale.reshape(1, -1), rhs)
    own = lax.all_to_all(sent, ("xh", "g"), 0, 0, tiled=True)
    other = lax.ppermute(own[:, 8:], "c", swap)
    whole, low, far = pl.pallas_call(
        product_kernel,
        out_shape=(jax.ShapeDtypeStruct((PEERS, 8, 128), F32),) * 3,
        scratch_shapes=[
            pltpu.VMEM((2 * HALF, DEPTH), BF16),
            pltpu.VMEM((DEPTH, 4 * HALF), BF16),
            pltpu.VMEM((4 * HALF, 64), BF16),
            pltpu.VMEM((TILES, 32, 128), F32),
            pltpu.VMEM((64, 2 * HALF), BF16),
            pltpu.VMEM((64, 2 * HALF), F32),
        ],
        compiler_params=pltpu.CompilerParams(vmem_limit_bytes=32 << 20),
        name="kernel_product",
    )(own, other)
    near = lax.ppermute(far, "c", swap)
    partial = pl.pallas_call(
        join_kernel,
        out_shape=jax.ShapeDtypeStruct((PEERS, 16, 128), F32),
        in_specs=[vmem] * 3,
        compiler_params=pltpu.CompilerParams(vmem_limit_bytes=8 << 20),
        name="join",
    )(whole, low, near)
    got = lax.all_to_all(partial, ("xh", "g"), 0, 0, tiled=True)
    row = lax.broadcasted_iota(jnp.int32, (8, 128), 0)
    pair = jnp.where(row < 4, outputscale[0], noise[0])
    return pl.pallas_call(
        finish_kernel,
        out_shape=(jax.ShapeDtypeStruct(rhs.shape, F32),) * 2,
        in_specs=[vmem] * 3,
        compiler_params=pltpu.CompilerParams(vmem_limit_bytes=8 << 20),
        name="update",
    )(got, rhs, pair)


def solution(mesh):
    split = Mesh(mesh.devices.reshape(CHIPS, 2, 2), ("g", "c", "xh"))
    vectors = P("xh", ("g", "c"))
    return jax.shard_map(
        on_device,
        mesh=split,
        in_specs=(P(("g", "c", "xh"), None), P(), P(), P(), P(), P(), vectors),
        out_specs=(vectors, vectors),
        check_vma=False,
    )
```

```python
import jax
import jax.numpy as jnp
from jax import lax
from jax.experimental import pallas as pl
from jax.experimental.pallas import tpu as pltpu
from jax.sharding import Mesh
from jax.sharding import PartitionSpec as P

F32, BF16 = jnp.float32, jnp.bfloat16
ROOT_LOG2E = 1.2011224087864498
CHIPS = 32
PEERS = 64
GROUPS = 8
WIDTH = 32
DEPTH = 256
STEPS = 4
ROWS = 256
PAIRS = [(a, b, t) for a in range(GROUPS) for b in range(a + 1, GROUPS) for t in range(2)]
TILES = CHIPS // 2
HALF = TILES * 128 // 2


def halves(x):
    high = x.astype(BF16)
    return high, (x - high.astype(F32)).astype(BF16)


def pack_kernel(
    enc_hbm, w1_hbm, w2_hbm, inv_hbm, rhs_hbm, out_ref,
    enc_ref, w1_ref, w2_ref, inv_ref, rhs_ref, set_ref, part_ref, big_sem, sem,
):
    small = [
        pltpu.make_async_copy(src, dst, sem.at[n])
        for n, (src, dst) in enumerate(
            ((w2_hbm, w2_ref), (inv_hbm, inv_ref), (rhs_hbm, rhs_ref))
        )
    ]
    depth = enc_hbm.shape[1] // STEPS
    big = []
    for n in range(STEPS):
        at = pl.ds(n * depth, depth)
        big.append(
            (
                pltpu.make_async_copy(enc_hbm.at[:, at], enc_ref.at[:, at], big_sem.at[2 * n]),
                pltpu.make_async_copy(w1_hbm.at[at], w1_ref.at[at], big_sem.at[2 * n + 1]),
            )
        )
    for pair in big:
        for copy in pair:
            copy.start()
    for copy in small:
        copy.start()
    hidden = jnp.zeros((enc_hbm.shape[0], w1_hbm.shape[1]), F32)
    for n in range(STEPS):
        at = slice(n * depth, (n + 1) * depth)
        for copy in big[n]:
            copy.wait()
        hidden = hidden + jnp.dot(enc_ref[:, at], w1_ref[at], preferred_element_type=F32)
    hidden = jnp.maximum(hidden, 0.0).astype(BF16)
    for copy in small:
        copy.wait()
    features = lax.dot_general(
        w2_ref[...], hidden, (((1,), (1,)), ((), ())), preferred_element_type=F32
    )
    n = features.shape[0]
    diagonal = lax.broadcasted_iota(jnp.int32, (n, n), 0) == lax.broadcasted_iota(
        jnp.int32, (n, n), 1
    )
    inv = jnp.sum(
        jnp.where(diagonal, jnp.broadcast_to(inv_ref[...], (n, n)), 0.0), axis=1, keepdims=True
    )
    features = features * inv * ROOT_LOG2E
    late = rhs_ref.shape[1] // 2
    for a in range(GROUPS):
        lo = WIDTH * a
        at, after = slice(lo, lo + WIDTH), slice(late + lo, late + lo + WIDTH)
        set_ref[a] = jnp.concatenate(
            [features[:16, at], features[16:, at], rhs_ref[:, at], rhs_ref[:, after]], axis=1
        )
        for t in range(2):
            lo = WIDTH * a + 16 * t
            at, after = slice(lo, lo + 16), slice(late + lo, late + lo + 16)
            part_ref[2 * a + t] = jnp.concatenate(
                [features[8 * m : 8 * m + 8, at] for m in range(4)]
                + [rhs_ref[8 * m : 8 * m + 8, s] for m in range(2) for s in (at, after)],
                axis=1,
            )
    for k, (a, b, t) in enumerate(PAIRS):
        out_ref[k, :16] = set_ref[a]
        out_ref[k, 16:] = part_ref[2 * b + t]
    for a in range(GROUPS):
        out_ref[len(PAIRS) + a, :8] = jnp.zeros((8, 128), F32)
        out_ref[len(PAIRS) + a, 8:] = set_ref[a]


def points_of(ref, k, lo):
    a0, a1 = ref[2 * k, lo : lo + 16], ref[2 * k + 1, lo : lo + 16]
    b0, b1 = ref[CHIPS + 2 * k, lo : lo + 16], ref[CHIPS + 2 * k + 1, lo : lo + 16]
    four = (a0, b0, a1, b1)
    features = jnp.concatenate(
        [
            jnp.concatenate([x[:, :32] for x in four], axis=1),
            jnp.concatenate([x[:, 32:64] for x in four], axis=1),
        ],
        axis=0,
    )
    columns = jnp.concatenate(
        [
            jnp.concatenate([a0[:, 64:], a1[:, 64:]], axis=1),
            jnp.concatenate([b0[:, 64:], b1[:, 64:]], axis=1),
        ],
        axis=0,
    )
    return features, columns


def half_points_of(ref, k, lo):
    units = [[ref[CHIPS * xh + 4 * k + j, lo : lo + 8] for xh in range(2)] for j in range(4)]
    features = jnp.concatenate(
        [
            jnp.concatenate([u[:, 16 * m : 16 * m + 16] for pair in units for u in pair], axis=1)
            for m in range(4)
        ],
        axis=0,
    )
    columns = jnp.concatenate(
        [
            jnp.concatenate([pair[xh][:, s : s + 32] for pair in units], axis=1)
            for xh in range(2)
            for s in (64, 96)
        ],
        axis=0,
    )
    return features, columns


def operand(features, left):
    y1, y2 = halves(features)
    kept = y1.astype(F32) + y2.astype(F32)
    norm = -0.5 * jnp.sum(kept * kept, axis=0, keepdims=True)
    n1 = norm.astype(BF16).astype(F32)
    n2 = (norm - n1).astype(BF16).astype(F32)
    n3 = norm - n1 - n2
    row = lax.broadcasted_iota(jnp.int32, (16, features.shape[1]), 0)
    own, other = (3, 0) if left else (0, 3)
    tail = jnp.where(
        row == own,
        n1,
        jnp.where(
            row == own + 1,
            n2,
            jnp.where(
                row == own + 2, n3, jnp.where((row >= other) & (row < other + 3), 1.0, 0.0)
            ),
        ),
    ).astype(BF16)
    blank = jnp.zeros((DEPTH - 144, features.shape[1]), BF16)
    parts = [y1, y1, y2, y2] if left else [y1, y2, y1, y2]
    return jnp.concatenate(parts + [tail, blank], axis=0)


def product_kernel(
    own_ref, other_ref, whole_ref, low_ref, far_ref,
    left_ref, right_ref, vec_ref, rows_ref, flat_ref, back_ref,
):
    on_pair = lax.axis_index("xh") * CHIPS + lax.axis_index("g") < len(PAIRS)
    core = lax.axis_index("c")
    lane = lax.broadcasted_iota(jnp.int32, (8, 128), 1)

    def set_rows(k, points):
        features, columns = points
        at = slice(k * 128, (k + 1) * 128)
        left_ref[at, :] = operand(features, True).T
        rows_ref[k] = columns
        flat_ref[:, at] = jnp.concatenate(halves(columns), axis=0)

    def set_columns(at, points):
        features, columns = points
        right_ref[:, at] = operand(features, False)
        vec_ref[at, :] = jnp.concatenate(halves(columns), axis=0).T

    def block(strip, at, back_from):
        exponent = jnp.dot(left_ref[strip, :], right_ref[:, at], preferred_element_type=F32)
        tile = jnp.exp2(exponent).astype(BF16)
        total = jnp.dot(tile, vec_ref[at, :], preferred_element_type=F32)
        if back_from < at.stop:
            back = jnp.dot(
                flat_ref[:, strip], tile[:, back_from - at.start :], preferred_element_type=F32
            )
            back_ref[:, back_from : at.stop] = back_ref[:, back_from : at.stop] + back
        return total

    def give_rows(k, image):
        for xh in range(2):
            top, low = image[16 * xh : 16 * xh + 8], image[16 * xh + 8 : 16 * xh + 16]
            for chip in range(2):
                at = slice(64 * chip, 64 * (chip + 1))
                whole_ref[CHIPS * xh + 2 * k + chip] = jnp.concatenate(
                    [top[:, at], low[:, at]], axis=1
                )

    def sums_of(product, square):
        here = jnp.zeros((8, 128), F32)
        for n, x in enumerate((product, square)):
            x = jnp.sum(x, axis=1, keepdims=True)
            for m in range(4):
                here = jnp.where(lane == 64 + 4 * (m // 2) + 2 * n + m % 2, x[8 * m : 8 * m + 8], here)
        return here

    back_ref[...] = jnp.zeros_like(back_ref)

    @pl.when(on_pair)
    def _():
        for k in range(TILES):
            set_rows(k, points_of(own_ref, k, 0))
        for n in range(TILES):
            ref, k, lo = (own_ref, n, 16) if n < TILES // 2 else (other_ref, n - TILES // 2, 8)
            set_columns(slice(128 * n, 128 * n + 128), half_points_of(ref, k, lo))
        product = jnp.zeros((32, 128), F32)
        for r in range(2 * HALF // ROWS):
            total = block(slice(ROWS * r, ROWS * (r + 1)), slice(0, 2 * HALF), 0)
            for n in range(ROWS // 128):
                k = ROWS // 128 * r + n
                both = total[128 * n : 128 * (n + 1)].T
                image = both[:32] + both[32:]
                product = product + 2.0 * (rows_ref[k] * image)
                give_rows(k, image)
        far_ref[PEERS] = sums_of(product, jnp.zeros((32, 128), F32))
        blank = jnp.zeros((8, 64), F32)
        for n in range(TILES):
            at = slice(n * 128, (n + 1) * 128)
            image = back_ref[:32, at] + back_ref[32:, at]
            k = n % (TILES // 2)
            ref = low_ref if n < TILES // 2 else far_ref
            for xh in range(2):
                for j in range(4):
                    at = slice(32 * j, 32 * j + 32)
                    ref[CHIPS * xh + 4 * k + j] = jnp.concatenate(
                        [
                            image[16 * xh : 16 * xh + 8, at],
                            image[16 * xh + 8 : 16 * xh + 16, at],
                            blank,
                        ],
                        axis=1,
                    )

    @pl.when(jnp.logical_not(on_pair))
    def _():
        for k in range(TILES):
            points = points_of(own_ref, k, 8)
            set_rows(k, points)
            set_columns(slice(128 * k, 128 * k + 128), points)
        for k in range(TILES):
            half = (k // (TILES // 2) + core) % 2
            at = 2 * HALF + half * HALF + k % (TILES // 2) * 128
            set_columns(pl.ds(pl.multiple_of(at, 128), 128), points_of(other_ref, k, 0))
        product = jnp.zeros((32, 128), F32)
        square = jnp.zeros((32, 128), F32)
        for r in range(2 * HALF // ROWS):
            strip = slice(ROWS * r, ROWS * (r + 1))
            near = block(strip, slice(strip.start, 2 * HALF), strip.stop)
            start = 2 * HALF + strip.start // HALF * HALF
            total = jnp.concatenate(
                [near, block(strip, slice(start, start + HALF), start)], axis=1
            )
            for n in range(ROWS // 128):
                k = ROWS // 128 * r + n
                at = slice(128 * k, 128 * (k + 1))
                four = total[128 * n : 128 * (n + 1)].T
                image = four[:32] + four[32:64] + (back_ref[:32, at] + back_ref[32:, at])
                cross = four[64:96] + four[96:]
                rows = rows_ref[k]
                product = product + rows * (image + 2.0 * cross)
                square = square + rows * rows
                give_rows(k, image + cross)
        far_ref[PEERS] = sums_of(product, square)
        low_ref[...] = jnp.zeros_like(low_ref)
        for k in range(TILES):
            half = (k // (TILES // 2) + core) % 2
            at = pl.multiple_of(2 * HALF + half * HALF + k % (TILES // 2) * 128, 128)
            both = back_ref[:, pl.ds(at, 128)]
            image = both[:32] + both[32:]
            for xh in range(2):
                top, low = image[16 * xh : 16 * xh + 8], image[16 * xh + 8 : 16 * xh + 16]
                for chip in range(2):
                    at = slice(64 * chip, 64 * (chip + 1))
                    far_ref[CHIPS * xh + 2 * k + chip] = jnp.concatenate(
                        [top[:, at], low[:, at]], axis=1
                    )


def join_kernel(whole_ref, low_ref, far_ref, near_ref, pair_ref, out_ref):
    on_pair = lax.axis_index("xh") * CHIPS + lax.axis_index("g") < len(PAIRS)
    lane = lax.broadcasted_iota(jnp.int32, (8, 128), 1)
    near = near_ref[:PEERS]
    sums = jnp.where(lane < 72, far_ref[PEERS] + near_ref[PEERS], pair_ref[...])
    out_ref[:, :8] = whole_ref[...] + jnp.where(on_pair, 0.0, near)
    out_ref[:, 8:] = low_ref[...] + jnp.where(on_pair, near, 0.0) + sums


def finish_kernel(got_ref, rhs_ref, sol_ref, res_ref):
    pair = got_ref[0, 8:]
    scale, noise = pair[0:1, 72:73], pair[0:1, 100:101]
    whole = [None] * GROUPS
    part = [None] * (2 * GROUPS)
    sums = got_ref[len(PAIRS), 8:]

    def plus(x, y):
        return y if x is None else x + y

    for k, (a, b, t) in enumerate(PAIRS):
        low = got_ref[k, 8:]
        whole[a] = plus(whole[a], got_ref[k, :8])
        part[2 * b + t] = plus(part[2 * b + t], low)
        sums = sums + low
    for a in range(GROUPS):
        whole[a] = plus(whole[a], got_ref[len(PAIRS) + a, :8])
        if a:
            sums = sums + got_ref[len(PAIRS) + a, 8:]
    mine = jnp.where(lax.axis_index("xh") == 0, sums[:, 64:68], sums[:, 68:72])
    product = jnp.concatenate([mine[:, 0:1], mine[:, 1:2]], axis=0)
    square = jnp.concatenate([mine[:, 2:3], mine[:, 3:4]], axis=0)
    step = square / (scale * product + noise * square)
    image = jnp.concatenate(
        [
            jnp.concatenate(
                [
                    x[:, 64 * m + 32 * h : 64 * m + 32 * h + 32]
                    for h in range(2)
                    for x in whole
                ],
                axis=1,
            )
            for m in range(2)
        ],
        axis=0,
    )
    blank = jnp.zeros((8, 16), F32)
    image = image + jnp.concatenate(
        [
            jnp.concatenate(
                [
                    blank if x is None else x[:, 32 * m + 16 * h : 32 * m + 16 * h + 16]
                    for h in range(2)
                    for x in part
                ],
                axis=1,
            )
            for m in range(2)
        ],
        axis=0,
    )
    direction = rhs_ref[...]
    sol_ref[...] = step * direction
    res_ref[...] = direction - step * (scale * image + noise * direction)


def on_device(encodings, first_weight, second_weight, inv_scale, outputscale, noise, rhs):
    hbm, vmem = pl.BlockSpec(memory_space=pltpu.HBM), pl.BlockSpec(memory_space=pltpu.VMEM)
    swap = [(0, 1), (1, 0)]
    sent = pl.pallas_call(
        pack_kernel,
        out_shape=jax.ShapeDtypeStruct((PEERS, 24, 128), F32),
        in_specs=[hbm] * 5,
        scratch_shapes=[
            pltpu.VMEM(encodings.shape, BF16),
            pltpu.VMEM(first_weight.shape, BF16),
            pltpu.VMEM(second_weight.shape[::-1], BF16),
            pltpu.VMEM((1, inv_scale.size), F32),
            pltpu.VMEM(rhs.shape, F32),
            pltpu.VMEM((GROUPS, 16, 128), F32),
            pltpu.VMEM((2 * GROUPS, 8, 128), F32),
            pltpu.SemaphoreType.DMA((2 * STEPS,)),
            pltpu.SemaphoreType.DMA((3,)),
        ],
        name="features",
    )(encodings, first_weight, second_weight.T, inv_scale.reshape(1, -1), rhs)
    own = lax.all_to_all(sent, ("xh", "g"), 0, 0, tiled=True)
    other = lax.ppermute(own[:, 8:], "c", swap)
    whole, low, far = pl.pallas_call(
        product_kernel,
        out_shape=tuple(jax.ShapeDtypeStruct((n, 8, 128), F32) for n in (PEERS, PEERS, PEERS + 1)),
        scratch_shapes=[
            pltpu.VMEM((2 * HALF, DEPTH), BF16),
            pltpu.VMEM((DEPTH, 4 * HALF), BF16),
            pltpu.VMEM((4 * HALF, 64), BF16),
            pltpu.VMEM((TILES, 32, 128), F32),
            pltpu.VMEM((64, 2 * HALF), BF16),
            pltpu.VMEM((64, 4 * HALF), F32),
        ],
        compiler_params=pltpu.CompilerParams(vmem_limit_bytes=32 << 20),
        name="kernel_product",
    )(own, other)
    near = lax.ppermute(far, "c", swap)
    lane = lax.broadcasted_iota(jnp.int32, (8, 128), 1)
    pair = jnp.where(lane < 72, 0.0, jnp.where(lane < 100, outputscale[0], noise[0]))
    partial = pl.pallas_call(
        join_kernel,
        out_shape=jax.ShapeDtypeStruct((PEERS, 16, 128), F32),
        in_specs=[vmem] * 5,
        compiler_params=pltpu.CompilerParams(vmem_limit_bytes=8 << 20),
        name="join",
    )(whole, low, far, near, pair)
    got = lax.all_to_all(partial, ("xh", "g"), 0, 0, tiled=True)
    return pl.pallas_call(
        finish_kernel,
        out_shape=(jax.ShapeDtypeStruct(rhs.shape, F32),) * 2,
        in_specs=[vmem] * 2,
        compiler_params=pltpu.CompilerParams(vmem_limit_bytes=8 << 20),
        name="update",
    )(got, rhs)


def solution(mesh):
    split = Mesh(mesh.devices.reshape(CHIPS, 2, 2), ("g", "c", "xh"))
    vectors = P("xh", ("g", "c"))
    return jax.shard_map(
        on_device,
        mesh=split,
        in_specs=(P(("g", "c", "xh"), None), P(), P(), P(), P(), P(), vectors),
        out_specs=(vectors, vectors),
        check_vma=False,
    )
```

```python
import jax
import jax.numpy as jnp
from jax import lax
from jax.experimental import pallas as pl
from jax.experimental.pallas import tpu as pltpu
from jax.sharding import Mesh
from jax.sharding import PartitionSpec as P

F32, BF16 = jnp.float32, jnp.bfloat16
ROOT_LOG2E = 1.2011224087864498
CHIPS = 32
PEERS = 64
GROUPS = 8
WIDTH = 32
DEPTH = 256
STEPS = 4
ROWS = 256
PAIRS = [(a, b, t) for a in range(GROUPS) for b in range(a + 1, GROUPS) for t in range(2)]
TILES = CHIPS // 2
HALF = TILES * 128 // 2


def halves(x):
    high = x.astype(BF16)
    return high, (x - high.astype(F32)).astype(BF16)


def pack_kernel(
    enc_hbm, w1_hbm, w2_hbm, inv_hbm, rhs_hbm, out_ref,
    enc_ref, w1_ref, w2_ref, inv_ref, rhs_ref, set_ref, part_ref, big_sem, sem,
):
    small = [
        pltpu.make_async_copy(src, dst, sem.at[n])
        for n, (src, dst) in enumerate(
            ((w2_hbm, w2_ref), (inv_hbm, inv_ref), (rhs_hbm, rhs_ref))
        )
    ]
    depth = enc_hbm.shape[1] // STEPS
    big = []
    for n in range(STEPS):
        at = pl.ds(n * depth, depth)
        big.append(
            (
                pltpu.make_async_copy(enc_hbm.at[:, at], enc_ref.at[:, at], big_sem.at[2 * n]),
                pltpu.make_async_copy(w1_hbm.at[at], w1_ref.at[at], big_sem.at[2 * n + 1]),
            )
        )
    for pair in big:
        for copy in pair:
            copy.start()
    for copy in small:
        copy.start()
    hidden = jnp.zeros((enc_hbm.shape[0], w1_hbm.shape[1]), F32)
    for n in range(STEPS):
        at = slice(n * depth, (n + 1) * depth)
        for copy in big[n]:
            copy.wait()
        hidden = hidden + jnp.dot(enc_ref[:, at], w1_ref[at], preferred_element_type=F32)
    hidden = jnp.maximum(hidden, 0.0).astype(BF16)
    for copy in small:
        copy.wait()
    features = lax.dot_general(
        w2_ref[...], hidden, (((1,), (1,)), ((), ())), preferred_element_type=F32
    )
    n = features.shape[0]
    diagonal = lax.broadcasted_iota(jnp.int32, (n, n), 0) == lax.broadcasted_iota(
        jnp.int32, (n, n), 1
    )
    inv = jnp.sum(
        jnp.where(diagonal, jnp.broadcast_to(inv_ref[...], (n, n)), 0.0), axis=1, keepdims=True
    )
    features = features * inv * ROOT_LOG2E
    late = rhs_ref.shape[1] // 2
    for a in range(GROUPS):
        lo = WIDTH * a
        at, after = slice(lo, lo + WIDTH), slice(late + lo, late + lo + WIDTH)
        set_ref[a] = jnp.concatenate(
            [features[:16, at], features[16:, at], rhs_ref[:, at], rhs_ref[:, after]], axis=1
        )
        for t in range(2):
            lo = WIDTH * a + 16 * t
            at, after = slice(lo, lo + 16), slice(late + lo, late + lo + 16)
            part_ref[2 * a + t] = jnp.concatenate(
                [features[8 * m : 8 * m + 8, at] for m in range(4)]
                + [rhs_ref[8 * m : 8 * m + 8, s] for m in range(2) for s in (at, after)],
                axis=1,
            )
    for k, (a, b, t) in enumerate(PAIRS):
        out_ref[k, :16] = set_ref[a]
        out_ref[k, 16:] = part_ref[2 * b + t]
    for a in range(GROUPS):
        out_ref[len(PAIRS) + a, :8] = jnp.zeros((8, 128), F32)
        out_ref[len(PAIRS) + a, 8:] = set_ref[a]


def points_of(ref, k, lo):
    a0, a1 = ref[2 * k, lo : lo + 16], ref[2 * k + 1, lo : lo + 16]
    b0, b1 = ref[CHIPS + 2 * k, lo : lo + 16], ref[CHIPS + 2 * k + 1, lo : lo + 16]
    four = (a0, b0, a1, b1)
    features = jnp.concatenate(
        [
            jnp.concatenate([x[:, :32] for x in four], axis=1),
            jnp.concatenate([x[:, 32:64] for x in four], axis=1),
        ],
        axis=0,
    )
    columns = jnp.concatenate(
        [
            jnp.concatenate([a0[:, 64:], a1[:, 64:]], axis=1),
            jnp.concatenate([b0[:, 64:], b1[:, 64:]], axis=1),
        ],
        axis=0,
    )
    return features, columns


def half_points_of(ref, k, lo):
    units = [[ref[CHIPS * xh + 4 * k + j, lo : lo + 8] for xh in range(2)] for j in range(4)]
    features = jnp.concatenate(
        [
            jnp.concatenate([u[:, 16 * m : 16 * m + 16] for pair in units for u in pair], axis=1)
            for m in range(4)
        ],
        axis=0,
    )
    columns = jnp.concatenate(
        [
            jnp.concatenate([pair[xh][:, s : s + 32] for pair in units], axis=1)
            for xh in range(2)
            for s in (64, 96)
        ],
        axis=0,
    )
    return features, columns


def operand(features, left):
    y1, y2 = halves(features)
    kept = y1.astype(F32) + y2.astype(F32)
    norm = -0.5 * jnp.sum(kept * kept, axis=0, keepdims=True)
    n1 = norm.astype(BF16).astype(F32)
    n2 = (norm - n1).astype(BF16).astype(F32)
    n3 = norm - n1 - n2
    row = lax.broadcasted_iota(jnp.int32, (16, features.shape[1]), 0)
    own, other = (3, 0) if left else (0, 3)
    tail = jnp.where(
        row == own,
        n1,
        jnp.where(
            row == own + 1,
            n2,
            jnp.where(
                row == own + 2, n3, jnp.where((row >= other) & (row < other + 3), 1.0, 0.0)
            ),
        ),
    ).astype(BF16)
    blank = jnp.zeros((DEPTH - 144, features.shape[1]), BF16)
    parts = [y1, y1, y2, y2] if left else [y1, y2, y1, y2]
    return jnp.concatenate(parts + [tail, blank], axis=0)


def on_pair():
    return lax.axis_index("xh") * CHIPS + lax.axis_index("g") < len(PAIRS)


def set_columns(right_ref, vec_ref, at, points):
    features, columns = points
    right_ref[:, at] = operand(features, False)
    vec_ref[at, :] = jnp.concatenate(halves(columns), axis=0).T


def block(left_ref, flat_ref, right_ref, vec_ref, back_ref, strip, at, back_from, first):
    exponent = jnp.dot(left_ref[strip, :], right_ref[:, at], preferred_element_type=F32)
    tile = jnp.exp2(exponent).astype(BF16)
    total = jnp.dot(tile, vec_ref[at, :], preferred_element_type=F32)
    if back_from < at.stop:
        to = slice(back_from, at.stop)
        back = jnp.dot(
            flat_ref[:, strip], tile[:, back_from - at.start :], preferred_element_type=F32
        )
        back_ref[:, to] = back if first else back_ref[:, to] + back
    return total


def near_kernel(
    own_ref, left_ref, rows_ref, flat_ref, image_ref, back_ref, right_ref, vec_ref
):
    pair = on_pair()

    def set_rows(k, points):
        features, columns = points
        at = slice(k * 128, (k + 1) * 128)
        left_ref[at, :] = operand(features, True).T
        rows_ref[k] = columns
        flat_ref[:, at] = jnp.concatenate(halves(columns), axis=0)

    def multiply(ranges):
        for r in range(2 * HALF // ROWS):
            strip = slice(ROWS * r, ROWS * (r + 1))
            at, back_from = ranges(strip)
            total = block(
                left_ref, flat_ref, right_ref, vec_ref, back_ref, strip, at, back_from, r == 0
            )
            for n in range(ROWS // 128):
                both = total[128 * n : 128 * (n + 1)].T
                image_ref[ROWS // 128 * r + n] = both[:32] + both[32:]

    @pl.when(pair)
    def _():
        for k in range(TILES):
            set_rows(k, points_of(own_ref, k, 0))
        for n in range(TILES // 2):
            at = slice(128 * n, 128 * n + 128)
            set_columns(right_ref, vec_ref, at, half_points_of(own_ref, n, 16))
        multiply(lambda strip: (slice(0, HALF), 0))

    @pl.when(jnp.logical_not(pair))
    def _():
        for k in range(TILES):
            points = points_of(own_ref, k, 8)
            set_rows(k, points)
            set_columns(right_ref, vec_ref, slice(128 * k, 128 * k + 128), points)
        multiply(lambda strip: (slice(strip.start, 2 * HALF), strip.stop))
        for k in range(ROWS // 128, TILES):
            at = slice(128 * k, 128 * (k + 1))
            image_ref[k] = image_ref[k] + (back_ref[:32, at] + back_ref[32:, at])


def far_kernel(
    other_ref, left_ref, rows_ref, flat_ref, image_ref, back_in_ref,
    whole_ref, low_ref, far_ref, right_ref, vec_ref, back_ref,
):
    pair = on_pair()
    core = lax.axis_index("c")
    lane = lax.broadcasted_iota(jnp.int32, (8, 128), 1)

    def multiply(columns_of, both_times, square_times):
        product = jnp.zeros((32, 128), F32)
        square = jnp.zeros((32, 128), F32)
        for r in range(2 * HALF // ROWS):
            strip = slice(ROWS * r, ROWS * (r + 1))
            at, first = columns_of(strip)
            total = block(
                left_ref, flat_ref, right_ref, vec_ref, back_ref, strip, at, at.start, first
            )
            for n in range(ROWS // 128):
                k = ROWS // 128 * r + n
                both = total[128 * n : 128 * (n + 1)].T
                cross = both[:32] + both[32:]
                rows = rows_ref[k]
                product = product + rows * (both_times * image_ref[k] + 2.0 * cross)
                if square_times:
                    square = square + rows * rows
                give_whole(whole_ref, k, image_ref[k] + cross)
        here = jnp.zeros((8, 128), F32)
        for n, x in enumerate((product, square)):
            x = jnp.sum(x, axis=1, keepdims=True)
            for m in range(4):
                to = 64 + 4 * (m // 2) + 2 * n + m % 2
                here = jnp.where(lane == to, x[8 * m : 8 * m + 8], here)
        far_ref[PEERS] = here

    def give_whole(ref, k, image):
        for xh in range(2):
            top, low = image[16 * xh : 16 * xh + 8], image[16 * xh + 8 : 16 * xh + 16]
            for chip in range(2):
                at = slice(64 * chip, 64 * (chip + 1))
                ref[CHIPS * xh + 2 * k + chip] = jnp.concatenate([top[:, at], low[:, at]], axis=1)

    @pl.when(pair)
    def _():
        for n in range(TILES // 2):
            at = slice(128 * n, 128 * n + 128)
            set_columns(right_ref, vec_ref, at, half_points_of(other_ref, n, 8))
        multiply(lambda strip: (slice(0, HALF), strip.start == 0), 2.0, 0)
        blank = jnp.zeros((8, 64), F32)
        for given, ref in ((back_in_ref, low_ref), (back_ref, far_ref)):
            for k in range(TILES // 2):
                at = slice(k * 128, (k + 1) * 128)
                image = given[:32, at] + given[32:, at]
                for xh in range(2):
                    top, low = image[16 * xh : 16 * xh + 8], image[16 * xh + 8 : 16 * xh + 16]
                    for j in range(4):
                        at = slice(32 * j, 32 * j + 32)
                        ref[CHIPS * xh + 4 * k + j] = jnp.concatenate(
                            [top[:, at], low[:, at], blank], axis=1
                        )

    @pl.when(jnp.logical_not(pair))
    def _():
        def place(k):
            half = (k // (TILES // 2) + core) % 2
            return pl.ds(pl.multiple_of(half * HALF + k % (TILES // 2) * 128, 128), 128)

        for k in range(TILES):
            set_columns(right_ref, vec_ref, place(k), points_of(other_ref, k, 0))

        def columns_of(strip):
            start = strip.start // HALF * HALF
            return slice(start, start + HALF), strip.start == start

        multiply(columns_of, 1.0, 1)
        low_ref[...] = jnp.zeros_like(low_ref)
        for k in range(TILES):
            both = back_ref[:, place(k)]
            give_whole(far_ref, k, both[:32] + both[32:])


def join_kernel(whole_ref, low_ref, far_ref, near_ref, scale_ref, noise_ref, out_ref):
    pair = on_pair()
    lane = lax.broadcasted_iota(jnp.int32, (8, 128), 1)
    near = near_ref[:PEERS]
    sums = jnp.where(
        lane < 72,
        far_ref[PEERS] + near_ref[PEERS],
        jnp.where(lane < 100, scale_ref[0], noise_ref[0]),
    )
    out_ref[:, :8] = whole_ref[...] + jnp.where(pair, 0.0, near)
    out_ref[:, 8:] = low_ref[...] + jnp.where(pair, near, 0.0) + sums


def finish_kernel(got_ref, rhs_ref, sol_ref, res_ref):
    pair = got_ref[0, 8:]
    scale, noise = pair[0:1, 72:73], pair[0:1, 100:101]
    whole = [None] * GROUPS
    part = [None] * (2 * GROUPS)
    sums = got_ref[len(PAIRS), 8:]

    def plus(x, y):
        return y if x is None else x + y

    for k, (a, b, t) in enumerate(PAIRS):
        low = got_ref[k, 8:]
        whole[a] = plus(whole[a], got_ref[k, :8])
        part[2 * b + t] = plus(part[2 * b + t], low)
        sums = sums + low
    for a in range(GROUPS):
        whole[a] = plus(whole[a], got_ref[len(PAIRS) + a, :8])
        if a:
            sums = sums + got_ref[len(PAIRS) + a, 8:]
    mine = jnp.where(lax.axis_index("xh") == 0, sums[:, 64:68], sums[:, 68:72])
    product = jnp.concatenate([mine[:, 0:1], mine[:, 1:2]], axis=0)
    square = jnp.concatenate([mine[:, 2:3], mine[:, 3:4]], axis=0)
    step = square / (scale * product + noise * square)
    image = jnp.concatenate(
        [
            jnp.concatenate(
                [
                    x[:, 64 * m + 32 * h : 64 * m + 32 * h + 32]
                    for h in range(2)
                    for x in whole
                ],
                axis=1,
            )
            for m in range(2)
        ],
        axis=0,
    )
    blank = jnp.zeros((8, 16), F32)
    image = image + jnp.concatenate(
        [
            jnp.concatenate(
                [
                    blank if x is None else x[:, 32 * m + 16 * h : 32 * m + 16 * h + 16]
                    for h in range(2)
                    for x in part
                ],
                axis=1,
            )
            for m in range(2)
        ],
        axis=0,
    )
    direction = rhs_ref[...]
    sol_ref[...] = step * direction
    res_ref[...] = direction - step * (scale * image + noise * direction)


def on_device(encodings, first_weight, second_weight, inv_scale, outputscale, noise, rhs):
    hbm, vmem = pl.BlockSpec(memory_space=pltpu.HBM), pl.BlockSpec(memory_space=pltpu.VMEM)
    swap = [(0, 1), (1, 0)]
    sent = pl.pallas_call(
        pack_kernel,
        out_shape=jax.ShapeDtypeStruct((PEERS, 24, 128), F32),
        in_specs=[hbm] * 5,
        scratch_shapes=[
            pltpu.VMEM(encodings.shape, BF16),
            pltpu.VMEM(first_weight.shape, BF16),
            pltpu.VMEM(second_weight.shape[::-1], BF16),
            pltpu.VMEM((1, inv_scale.size), F32),
            pltpu.VMEM(rhs.shape, F32),
            pltpu.VMEM((GROUPS, 16, 128), F32),
            pltpu.VMEM((2 * GROUPS, 8, 128), F32),
            pltpu.SemaphoreType.DMA((2 * STEPS,)),
            pltpu.SemaphoreType.DMA((3,)),
        ],
        name="features",
    )(encodings, first_weight, second_weight.T, inv_scale.reshape(1, -1), rhs)
    own = lax.all_to_all(sent, ("xh", "g"), 0, 0, tiled=True)
    other = lax.ppermute(own[:, 8:], "c", swap)
    cost = pl.CostEstimate(flops=4 << 30, bytes_accessed=1 << 20, transcendentals=1 << 21)
    *rows, back = pl.pallas_call(
        near_kernel,
        out_shape=(
            jax.ShapeDtypeStruct((2 * HALF, DEPTH), BF16),
            jax.ShapeDtypeStruct((TILES, 32, 128), F32),
            jax.ShapeDtypeStruct((64, 2 * HALF), BF16),
            jax.ShapeDtypeStruct((TILES, 32, 128), F32),
            jax.ShapeDtypeStruct((64, 2 * HALF), F32),
        ),
        scratch_shapes=[
            pltpu.VMEM((DEPTH, 2 * HALF), BF16),
            pltpu.VMEM((2 * HALF, 64), BF16),
        ],
        compiler_params=pltpu.CompilerParams(vmem_limit_bytes=24 << 20),
        cost_estimate=cost,
        name="own_columns",
    )(own)
    whole, low, far = pl.pallas_call(
        far_kernel,
        out_shape=tuple(jax.ShapeDtypeStruct((n, 8, 128), F32) for n in (PEERS, PEERS, PEERS + 1)),
        scratch_shapes=[
            pltpu.VMEM((DEPTH, 2 * HALF), BF16),
            pltpu.VMEM((2 * HALF, 64), BF16),
            pltpu.VMEM((64, 2 * HALF), F32),
        ],
        compiler_params=pltpu.CompilerParams(vmem_limit_bytes=24 << 20),
        cost_estimate=cost,
        name="other_columns",
    )(other, *rows, back)
    near = lax.ppermute(far, "c", swap)
    smem = pl.BlockSpec(memory_space=pltpu.SMEM)
    partial = pl.pallas_call(
        join_kernel,
        out_shape=jax.ShapeDtypeStruct((PEERS, 16, 128), F32),
        in_specs=[vmem] * 4 + [smem] * 2,
        compiler_params=pltpu.CompilerParams(vmem_limit_bytes=8 << 20),
        name="join",
    )(whole, low, far, near, outputscale, noise)
    got = lax.all_to_all(partial, ("xh", "g"), 0, 0, tiled=True)
    return pl.pallas_call(
        finish_kernel,
        out_shape=(jax.ShapeDtypeStruct(rhs.shape, F32),) * 2,
        in_specs=[vmem] * 2,
        compiler_params=pltpu.CompilerParams(vmem_limit_bytes=8 << 20),
        name="update",
    )(got, rhs)


def solution(mesh):
    split = Mesh(mesh.devices.reshape(CHIPS, 2, 2), ("g", "c", "xh"))
    vectors = P("xh", ("g", "c"))
    return jax.shard_map(
        on_device,
        mesh=split,
        in_specs=(P(("g", "c", "xh"), None), P(), P(), P(), P(), P(), vectors),
        out_specs=(vectors, vectors),
        check_vma=False,
    )
```

```python
import jax
import jax.numpy as jnp
from jax import lax
from jax.experimental import pallas as pl
from jax.experimental.pallas import tpu as pltpu
from jax.sharding import Mesh
from jax.sharding import PartitionSpec as P

F32, BF16 = jnp.float32, jnp.bfloat16
ROOT_LOG2E = 1.2011224087864498
CHIPS = 32
PEERS = 64
GROUPS = 8
WIDTH = 32
DEPTH = 256
STEPS = 4
ROWS = 256
PAIR_ROWS = 512
AHEAD = 0
PAIRS = [(a, b, t) for a in range(GROUPS) for b in range(a + 1, GROUPS) for t in range(2)]
TILES = CHIPS // 2
HALF = TILES * 128 // 2


def halves(x):
    high = x.astype(BF16)
    return high, (x - high.astype(F32)).astype(BF16)


def pack_kernel(
    enc_hbm, w1_hbm, w2_hbm, inv_hbm, rhs_hbm, out_ref,
    enc_ref, w1_ref, w2_ref, inv_ref, rhs_ref, set_ref, part_ref, big_sem, sem,
):
    small = [
        pltpu.make_async_copy(src, dst, sem.at[n])
        for n, (src, dst) in enumerate(
            ((w2_hbm, w2_ref), (inv_hbm, inv_ref), (rhs_hbm, rhs_ref))
        )
    ]
    depth = enc_hbm.shape[1] // STEPS
    big = []
    for n in range(STEPS):
        at = pl.ds(n * depth, depth)
        big.append(
            (
                pltpu.make_async_copy(enc_hbm.at[:, at], enc_ref.at[:, at], big_sem.at[2 * n]),
                pltpu.make_async_copy(w1_hbm.at[at], w1_ref.at[at], big_sem.at[2 * n + 1]),
            )
        )
    for pair in big:
        for copy in pair:
            copy.start()
    for copy in small:
        copy.start()
    hidden = jnp.zeros((enc_hbm.shape[0], w1_hbm.shape[1]), F32)
    for n in range(STEPS):
        at = slice(n * depth, (n + 1) * depth)
        for copy in big[n]:
            copy.wait()
        hidden = hidden + jnp.dot(enc_ref[:, at], w1_ref[at], preferred_element_type=F32)
    hidden = jnp.maximum(hidden, 0.0).astype(BF16)
    for copy in small:
        copy.wait()
    features = lax.dot_general(
        w2_ref[...], hidden, (((1,), (1,)), ((), ())), preferred_element_type=F32
    )
    n = features.shape[0]
    diagonal = lax.broadcasted_iota(jnp.int32, (n, n), 0) == lax.broadcasted_iota(
        jnp.int32, (n, n), 1
    )
    inv = jnp.sum(
        jnp.where(diagonal, jnp.broadcast_to(inv_ref[...], (n, n)), 0.0), axis=1, keepdims=True
    )
    features = features * inv * ROOT_LOG2E
    late = rhs_ref.shape[1] // 2
    for a in range(GROUPS):
        lo = WIDTH * a
        at, after = slice(lo, lo + WIDTH), slice(late + lo, late + lo + WIDTH)
        set_ref[a] = jnp.concatenate(
            [features[:16, at], features[16:, at], rhs_ref[:, at], rhs_ref[:, after]], axis=1
        )
        for t in range(2):
            lo = WIDTH * a + 16 * t
            at, after = slice(lo, lo + 16), slice(late + lo, late + lo + 16)
            part_ref[2 * a + t] = jnp.concatenate(
                [features[8 * m : 8 * m + 8, at] for m in range(4)]
                + [rhs_ref[8 * m : 8 * m + 8, s] for m in range(2) for s in (at, after)],
                axis=1,
            )
    for k, (a, b, t) in enumerate(PAIRS):
        out_ref[k, :16] = set_ref[a]
        out_ref[k, 16:] = part_ref[2 * b + t]
    for a in range(GROUPS):
        out_ref[len(PAIRS) + a, :8] = jnp.zeros((8, 128), F32)
        out_ref[len(PAIRS) + a, 8:] = set_ref[a]


def points_of(ref, k, lo):
    a0, a1 = ref[2 * k, lo : lo + 16], ref[2 * k + 1, lo : lo + 16]
    b0, b1 = ref[CHIPS + 2 * k, lo : lo + 16], ref[CHIPS + 2 * k + 1, lo : lo + 16]
    four = (a0, b0, a1, b1)
    features = jnp.concatenate(
        [
            jnp.concatenate([x[:, :32] for x in four], axis=1),
            jnp.concatenate([x[:, 32:64] for x in four], axis=1),
        ],
        axis=0,
    )
    columns = jnp.concatenate(
        [
            jnp.concatenate([a0[:, 64:], a1[:, 64:]], axis=1),
            jnp.concatenate([b0[:, 64:], b1[:, 64:]], axis=1),
        ],
        axis=0,
    )
    return features, columns


def half_points_of(ref, k, lo):
    units = [[ref[CHIPS * xh + 4 * k + j, lo : lo + 8] for xh in range(2)] for j in range(4)]
    features = jnp.concatenate(
        [
            jnp.concatenate([u[:, 16 * m : 16 * m + 16] for pair in units for u in pair], axis=1)
            for m in range(4)
        ],
        axis=0,
    )
    columns = jnp.concatenate(
        [
            jnp.concatenate([pair[xh][:, s : s + 32] for pair in units], axis=1)
            for xh in range(2)
            for s in (64, 96)
        ],
        axis=0,
    )
    return features, columns


def operand(features, left):
    y1, y2 = halves(features)
    kept = y1.astype(F32) + y2.astype(F32)
    norm = -0.5 * jnp.sum(kept * kept, axis=0, keepdims=True)
    n1 = norm.astype(BF16).astype(F32)
    n2 = (norm - n1).astype(BF16).astype(F32)
    n3 = norm - n1 - n2
    row = lax.broadcasted_iota(jnp.int32, (16, features.shape[1]), 0)
    own, other = (3, 0) if left else (0, 3)
    tail = jnp.where(
        row == own,
        n1,
        jnp.where(
            row == own + 1,
            n2,
            jnp.where(
                row == own + 2, n3, jnp.where((row >= other) & (row < other + 3), 1.0, 0.0)
            ),
        ),
    ).astype(BF16)
    blank = jnp.zeros((DEPTH - 144, features.shape[1]), BF16)
    parts = [y1, y1, y2, y2] if left else [y1, y2, y1, y2]
    return jnp.concatenate(parts + [tail, blank], axis=0)


def on_pair():
    return lax.axis_index("xh") * CHIPS + lax.axis_index("g") < len(PAIRS)


def set_columns(right_ref, vec_ref, at, points):
    features, columns = points
    right_ref[:, at] = operand(features, False)
    vec_ref[at, :] = jnp.concatenate(halves(columns), axis=0).T


def block(left_ref, flat_ref, right_ref, vec_ref, back_ref, strip, at, back_from, first):
    exponent = jnp.dot(left_ref[strip, :], right_ref[:, at], preferred_element_type=F32)
    tile = jnp.exp2(exponent).astype(BF16)
    total = jnp.dot(tile, vec_ref[at, :], preferred_element_type=F32)
    if back_from < at.stop:
        to = slice(back_from, at.stop)
        back = jnp.dot(
            flat_ref[:, strip], tile[:, back_from - at.start :], preferred_element_type=F32
        )
        back_ref[:, to] = back if first else back_ref[:, to] + back
    return total


def near_kernel(
    own_ref, left_ref, rows_ref, flat_ref, image_ref, back_ref, right_ref, vec_ref
):
    pair = on_pair()

    def set_rows(k, points):
        features, columns = points
        at = slice(k * 128, (k + 1) * 128)
        left_ref[at, :] = operand(features, True).T
        rows_ref[k] = columns
        flat_ref[:, at] = jnp.concatenate(halves(columns), axis=0)

    def multiply(rows, prepare, ranges):
        for r in range(2 * HALF // rows):
            strip = slice(rows * r, rows * (r + 1))
            ahead = strip.stop + AHEAD
            for k in range((strip.start + AHEAD if r else 0) // 128, min(ahead, 2 * HALF) // 128):
                prepare(k)
            at, back_from = ranges(strip)
            total = block(
                left_ref, flat_ref, right_ref, vec_ref, back_ref, strip, at, back_from, r == 0
            )
            for n in range(rows // 128):
                both = total[128 * n : 128 * (n + 1)].T
                image_ref[rows // 128 * r + n] = both[:32] + both[32:]

    @pl.when(pair)
    def _():
        for n in range(TILES // 2):
            at = slice(128 * n, 128 * n + 128)
            set_columns(right_ref, vec_ref, at, half_points_of(own_ref, n, 16))
        multiply(
            PAIR_ROWS,
            lambda k: set_rows(k, points_of(own_ref, k, 0)),
            lambda strip: (slice(0, HALF), 0),
        )

    @pl.when(jnp.logical_not(pair))
    def _():
        for k in range(TILES):
            points = points_of(own_ref, k, 8)
            set_rows(k, points)
            set_columns(right_ref, vec_ref, slice(128 * k, 128 * k + 128), points)
        multiply(
            ROWS, lambda k: None, lambda strip: (slice(strip.start, 2 * HALF), strip.stop)
        )
        for k in range(ROWS // 128, TILES):
            at = slice(128 * k, 128 * (k + 1))
            image_ref[k] = image_ref[k] + (back_ref[:32, at] + back_ref[32:, at])


def far_kernel(
    other_ref, left_ref, rows_ref, flat_ref, image_ref, back_in_ref,
    whole_ref, low_ref, far_ref, right_ref, vec_ref, back_ref,
):
    pair = on_pair()
    core = lax.axis_index("c")
    lane = lax.broadcasted_iota(jnp.int32, (8, 128), 1)

    def multiply(step, columns_of, both_times, square_times, beside=None):
        product = jnp.zeros((32, 128), F32)
        square = jnp.zeros((32, 128), F32)
        for r in range(2 * HALF // step):
            strip = slice(step * r, step * (r + 1))
            at, first = columns_of(strip)
            if beside is not None:
                beside(r, 2 * HALF // step)
            total = block(
                left_ref, flat_ref, right_ref, vec_ref, back_ref, strip, at, at.start, first
            )
            for n in range(step // 128):
                k = step // 128 * r + n
                both = total[128 * n : 128 * (n + 1)].T
                cross = both[:32] + both[32:]
                rows = rows_ref[k]
                product = product + rows * (both_times * image_ref[k] + 2.0 * cross)
                if square_times:
                    square = square + rows * rows
                give_whole(whole_ref, k, image_ref[k] + cross)
        here = jnp.zeros((8, 128), F32)
        for n, x in enumerate((product, square)):
            x = jnp.sum(x, axis=1, keepdims=True)
            for m in range(4):
                to = 64 + 4 * (m // 2) + 2 * n + m % 2
                here = jnp.where(lane == to, x[8 * m : 8 * m + 8], here)
        far_ref[PEERS] = here

    def give_whole(ref, k, image):
        for xh in range(2):
            top, low = image[16 * xh : 16 * xh + 8], image[16 * xh + 8 : 16 * xh + 16]
            for chip in range(2):
                at = slice(64 * chip, 64 * (chip + 1))
                ref[CHIPS * xh + 2 * k + chip] = jnp.concatenate([top[:, at], low[:, at]], axis=1)

    @pl.when(pair)
    def _():
        for n in range(TILES // 2):
            at = slice(128 * n, 128 * n + 128)
            set_columns(right_ref, vec_ref, at, half_points_of(other_ref, n, 8))
        blank = jnp.zeros((8, 64), F32)

        def give_part(given, ref, k):
            at = slice(k * 128, (k + 1) * 128)
            image = given[:32, at] + given[32:, at]
            for xh in range(2):
                top, low = image[16 * xh : 16 * xh + 8], image[16 * xh + 8 : 16 * xh + 16]
                for j in range(4):
                    at = slice(32 * j, 32 * j + 32)
                    ref[CHIPS * xh + 4 * k + j] = jnp.concatenate(
                        [top[:, at], low[:, at], blank], axis=1
                    )

        def beside(r, steps):
            for k in range(r * (TILES // 2) // steps, (r + 1) * (TILES // 2) // steps):
                give_part(back_in_ref, low_ref, k)

        multiply(PAIR_ROWS, lambda strip: (slice(0, HALF), strip.start == 0), 2.0, 0, beside)
        for k in range(TILES // 2):
            give_part(back_ref, far_ref, k)

    @pl.when(jnp.logical_not(pair))
    def _():
        def place(k):
            half = (k // (TILES // 2) + core) % 2
            return pl.ds(pl.multiple_of(half * HALF + k % (TILES // 2) * 128, 128), 128)

        for k in range(TILES):
            set_columns(right_ref, vec_ref, place(k), points_of(other_ref, k, 0))

        def columns_of(strip):
            start = strip.start // HALF * HALF
            return slice(start, start + HALF), strip.start == start

        multiply(ROWS, columns_of, 1.0, 1)
        low_ref[...] = jnp.zeros_like(low_ref)
        for k in range(TILES):
            both = back_ref[:, place(k)]
            give_whole(far_ref, k, both[:32] + both[32:])


def join_kernel(whole_ref, low_ref, far_ref, near_ref, scale_ref, noise_ref, out_ref):
    pair = on_pair()
    lane = lax.broadcasted_iota(jnp.int32, (8, 128), 1)
    near = near_ref[:PEERS]
    sums = jnp.where(
        lane < 72,
        far_ref[PEERS] + near_ref[PEERS],
        jnp.where(lane < 100, scale_ref[0], noise_ref[0]),
    )
    out_ref[:, :8] = whole_ref[...] + jnp.where(pair, 0.0, near)
    out_ref[:, 8:] = low_ref[...] + jnp.where(pair, near, 0.0) + sums


def finish_kernel(got_ref, rhs_ref, sol_ref, res_ref):
    pair = got_ref[0, 8:]
    scale, noise = pair[0:1, 72:73], pair[0:1, 100:101]
    whole = [None] * GROUPS
    part = [None] * (2 * GROUPS)
    sums = got_ref[len(PAIRS), 8:]

    def plus(x, y):
        return y if x is None else x + y

    for k, (a, b, t) in enumerate(PAIRS):
        low = got_ref[k, 8:]
        whole[a] = plus(whole[a], got_ref[k, :8])
        part[2 * b + t] = plus(part[2 * b + t], low)
        sums = sums + low
    for a in range(GROUPS):
        whole[a] = plus(whole[a], got_ref[len(PAIRS) + a, :8])
        if a:
            sums = sums + got_ref[len(PAIRS) + a, 8:]
    mine = jnp.where(lax.axis_index("xh") == 0, sums[:, 64:68], sums[:, 68:72])
    product = jnp.concatenate([mine[:, 0:1], mine[:, 1:2]], axis=0)
    square = jnp.concatenate([mine[:, 2:3], mine[:, 3:4]], axis=0)
    step = square / (scale * product + noise * square)
    image = jnp.concatenate(
        [
            jnp.concatenate(
                [
                    x[:, 64 * m + 32 * h : 64 * m + 32 * h + 32]
                    for h in range(2)
                    for x in whole
                ],
                axis=1,
            )
            for m in range(2)
        ],
        axis=0,
    )
    blank = jnp.zeros((8, 16), F32)
    image = image + jnp.concatenate(
        [
            jnp.concatenate(
                [
                    blank if x is None else x[:, 32 * m + 16 * h : 32 * m + 16 * h + 16]
                    for h in range(2)
                    for x in part
                ],
                axis=1,
            )
            for m in range(2)
        ],
        axis=0,
    )
    direction = rhs_ref[...]
    sol_ref[...] = step * direction
    res_ref[...] = direction - step * (scale * image + noise * direction)


def on_device(encodings, first_weight, second_weight, inv_scale, outputscale, noise, rhs):
    hbm, vmem = pl.BlockSpec(memory_space=pltpu.HBM), pl.BlockSpec(memory_space=pltpu.VMEM)
    swap = [(0, 1), (1, 0)]
    sent = pl.pallas_call(
        pack_kernel,
        out_shape=pltpu.VMEM((PEERS, 24, 128), F32),
        in_specs=[hbm] * 5,
        scratch_shapes=[
            pltpu.VMEM(encodings.shape, BF16),
            pltpu.VMEM(first_weight.shape, BF16),
            pltpu.VMEM(second_weight.shape[::-1], BF16),
            pltpu.VMEM((1, inv_scale.size), F32),
            pltpu.VMEM(rhs.shape, F32),
            pltpu.VMEM((GROUPS, 16, 128), F32),
            pltpu.VMEM((2 * GROUPS, 8, 128), F32),
            pltpu.SemaphoreType.DMA((2 * STEPS,)),
            pltpu.SemaphoreType.DMA((3,)),
        ],
        name="features",
    )(encodings, first_weight, second_weight.T, inv_scale.reshape(1, -1), rhs)
    own = lax.all_to_all(sent, ("xh", "g"), 0, 0, tiled=True)
    other = lax.ppermute(own[:, 8:], "c", swap)
    cost = pl.CostEstimate(flops=4 << 30, bytes_accessed=1 << 20, transcendentals=1 << 21)
    *rows, back = pl.pallas_call(
        near_kernel,
        out_shape=(
            jax.ShapeDtypeStruct((2 * HALF, DEPTH), BF16),
            jax.ShapeDtypeStruct((TILES, 32, 128), F32),
            jax.ShapeDtypeStruct((64, 2 * HALF), BF16),
            jax.ShapeDtypeStruct((TILES, 32, 128), F32),
            jax.ShapeDtypeStruct((64, 2 * HALF), F32),
        ),
        scratch_shapes=[
            pltpu.VMEM((DEPTH, 2 * HALF), BF16),
            pltpu.VMEM((2 * HALF, 64), BF16),
        ],
        compiler_params=pltpu.CompilerParams(vmem_limit_bytes=24 << 20),
        cost_estimate=cost,
        name="own_columns",
    )(own)
    whole, low, far = pl.pallas_call(
        far_kernel,
        out_shape=tuple(jax.ShapeDtypeStruct((n, 8, 128), F32) for n in (PEERS, PEERS, PEERS + 1)),
        scratch_shapes=[
            pltpu.VMEM((DEPTH, 2 * HALF), BF16),
            pltpu.VMEM((2 * HALF, 64), BF16),
            pltpu.VMEM((64, 2 * HALF), F32),
        ],
        compiler_params=pltpu.CompilerParams(vmem_limit_bytes=24 << 20),
        cost_estimate=cost,
        name="other_columns",
    )(other, *rows, back)
    near = lax.ppermute(far, "c", swap)
    smem = pl.BlockSpec(memory_space=pltpu.SMEM)
    partial = pl.pallas_call(
        join_kernel,
        out_shape=jax.ShapeDtypeStruct((PEERS, 16, 128), F32),
        in_specs=[vmem] * 4 + [smem] * 2,
        compiler_params=pltpu.CompilerParams(vmem_limit_bytes=8 << 20),
        name="join",
    )(whole, low, far, near, outputscale, noise)
    got = lax.all_to_all(partial, ("xh", "g"), 0, 0, tiled=True)
    return pl.pallas_call(
        finish_kernel,
        out_shape=(jax.ShapeDtypeStruct(rhs.shape, F32),) * 2,
        in_specs=[vmem] * 2,
        compiler_params=pltpu.CompilerParams(vmem_limit_bytes=8 << 20),
        name="update",
    )(got, rhs)


def solution(mesh):
    split = Mesh(mesh.devices.reshape(CHIPS, 2, 2), ("g", "c", "xh"))
    vectors = P("xh", ("g", "c"))
    return jax.shard_map(
        on_device,
        mesh=split,
        in_specs=(P(("g", "c", "xh"), None), P(), P(), P(), P(), P(), vectors),
        out_specs=(vectors, vectors),
        check_vma=False,
    )
```

```python
import jax
import jax.numpy as jnp
from jax import lax
from jax.experimental import pallas as pl
from jax.experimental.pallas import tpu as pltpu
from jax.sharding import Mesh
from jax.sharding import PartitionSpec as P

F32, BF16 = jnp.float32, jnp.bfloat16
ROOT_LOG2E = 1.2011224087864498
CHIPS = 32
PEERS = 64
GROUPS = 8
WIDTH = 32
DEPTH = 256
SHALLOW = 144
STEPS = 4
ROWS = 256
PAIR_ROWS = 512
AHEAD = 0
PAIRS = [(a, b, t) for a in range(GROUPS) for b in range(a + 1, GROUPS) for t in range(2)]
TILES = CHIPS // 2
HALF = TILES * 128 // 2


def halves(x):
    high = x.astype(BF16)
    return high, (x - high.astype(F32)).astype(BF16)


def pack_kernel(
    enc_hbm, w1_hbm, w2_hbm, inv_hbm, rhs_hbm, out_ref,
    enc_ref, w1_ref, w2_ref, inv_ref, rhs_ref, set_ref, part_ref, big_sem, sem,
):
    small = [
        pltpu.make_async_copy(src, dst, sem.at[n])
        for n, (src, dst) in enumerate(
            ((w2_hbm, w2_ref), (inv_hbm, inv_ref), (rhs_hbm, rhs_ref))
        )
    ]
    depth = enc_hbm.shape[1] // STEPS
    big = []
    for n in range(STEPS):
        at = pl.ds(n * depth, depth)
        big.append(
            (
                pltpu.make_async_copy(enc_hbm.at[:, at], enc_ref.at[:, at], big_sem.at[2 * n]),
                pltpu.make_async_copy(w1_hbm.at[at], w1_ref.at[at], big_sem.at[2 * n + 1]),
            )
        )
    for pair in big:
        for copy in pair:
            copy.start()
    for copy in small:
        copy.start()
    hidden = jnp.zeros((enc_hbm.shape[0], w1_hbm.shape[1]), F32)
    for n in range(STEPS):
        at = slice(n * depth, (n + 1) * depth)
        for copy in big[n]:
            copy.wait()
        hidden = hidden + jnp.dot(enc_ref[:, at], w1_ref[at], preferred_element_type=F32)
    hidden = jnp.maximum(hidden, 0.0).astype(BF16)
    for copy in small:
        copy.wait()
    features = lax.dot_general(
        w2_ref[...], hidden, (((1,), (1,)), ((), ())), preferred_element_type=F32
    )
    n = features.shape[0]
    diagonal = lax.broadcasted_iota(jnp.int32, (n, n), 0) == lax.broadcasted_iota(
        jnp.int32, (n, n), 1
    )
    inv = jnp.sum(
        jnp.where(diagonal, jnp.broadcast_to(inv_ref[...], (n, n)), 0.0), axis=1, keepdims=True
    )
    features = features * inv * ROOT_LOG2E
    late = rhs_ref.shape[1] // 2
    for a in range(GROUPS):
        lo = WIDTH * a
        at, after = slice(lo, lo + WIDTH), slice(late + lo, late + lo + WIDTH)
        set_ref[a] = jnp.concatenate(
            [features[:16, at], features[16:, at], rhs_ref[:, at], rhs_ref[:, after]], axis=1
        )
        for t in range(2):
            lo = WIDTH * a + 16 * t
            at, after = slice(lo, lo + 16), slice(late + lo, late + lo + 16)
            part_ref[2 * a + t] = jnp.concatenate(
                [features[8 * m : 8 * m + 8, at] for m in range(4)]
                + [rhs_ref[8 * m : 8 * m + 8, s] for m in range(2) for s in (at, after)],
                axis=1,
            )
    for k, (a, b, t) in enumerate(PAIRS):
        out_ref[k, :16] = set_ref[a]
        out_ref[k, 16:] = part_ref[2 * b + t]
    for a in range(GROUPS):
        out_ref[len(PAIRS) + a, :8] = jnp.zeros((8, 128), F32)
        out_ref[len(PAIRS) + a, 8:] = set_ref[a]


def points_of(ref, k, lo):
    a0, a1 = ref[2 * k, lo : lo + 16], ref[2 * k + 1, lo : lo + 16]
    b0, b1 = ref[CHIPS + 2 * k, lo : lo + 16], ref[CHIPS + 2 * k + 1, lo : lo + 16]
    four = (a0, b0, a1, b1)
    features = jnp.concatenate(
        [
            jnp.concatenate([x[:, :32] for x in four], axis=1),
            jnp.concatenate([x[:, 32:64] for x in four], axis=1),
        ],
        axis=0,
    )
    columns = jnp.concatenate(
        [
            jnp.concatenate([a0[:, 64:], a1[:, 64:]], axis=1),
            jnp.concatenate([b0[:, 64:], b1[:, 64:]], axis=1),
        ],
        axis=0,
    )
    return features, columns


def half_points_of(ref, k, lo):
    units = [[ref[CHIPS * xh + 4 * k + j, lo : lo + 8] for xh in range(2)] for j in range(4)]
    features = jnp.concatenate(
        [
            jnp.concatenate([u[:, 16 * m : 16 * m + 16] for pair in units for u in pair], axis=1)
            for m in range(4)
        ],
        axis=0,
    )
    columns = jnp.concatenate(
        [
            jnp.concatenate([pair[xh][:, s : s + 32] for pair in units], axis=1)
            for xh in range(2)
            for s in (64, 96)
        ],
        axis=0,
    )
    return features, columns


def operand(features, left, depth):
    y1, y2 = halves(features)
    kept = y1.astype(F32) + y2.astype(F32)
    norm = -0.5 * jnp.sum(kept * kept, axis=0, keepdims=True)
    n1 = norm.astype(BF16).astype(F32)
    n2 = (norm - n1).astype(BF16).astype(F32)
    n3 = norm - n1 - n2
    row = lax.broadcasted_iota(jnp.int32, (16, features.shape[1]), 0)
    own, other = (3, 0) if left else (0, 3)
    tail = jnp.where(
        row == own,
        n1,
        jnp.where(
            row == own + 1,
            n2,
            jnp.where(
                row == own + 2, n3, jnp.where((row >= other) & (row < other + 3), 1.0, 0.0)
            ),
        ),
    ).astype(BF16)
    parts = ([y1, y1, y2, y2] if left else [y1, y2, y1, y2]) + [tail]
    if depth > SHALLOW:
        parts.append(jnp.zeros((depth - SHALLOW, features.shape[1]), BF16))
    return jnp.concatenate(parts, axis=0)


def on_pair():
    return lax.axis_index("xh") * CHIPS + lax.axis_index("g") < len(PAIRS)


def set_columns(right_ref, vec_ref, at, points, depth):
    features, columns = points
    right_ref[:depth, at] = operand(features, False, depth)
    vec_ref[at, :] = jnp.concatenate(halves(columns), axis=0).T


def block(depth, left_ref, flat_ref, right_ref, vec_ref, back_ref, strip, at, back_from, first):
    exponent = jnp.dot(
        left_ref[strip, :depth], right_ref[:depth, at], preferred_element_type=F32
    )
    tile = jnp.exp2(exponent).astype(BF16)
    total = jnp.dot(tile, vec_ref[at, :], preferred_element_type=F32)
    if back_from < at.stop:
        to = slice(back_from, at.stop)
        back = jnp.dot(
            flat_ref[:, strip], tile[:, back_from - at.start :], preferred_element_type=F32
        )
        back_ref[:, to] = back if first else back_ref[:, to] + back
    return total


def near_kernel(
    own_ref, left_ref, rows_ref, flat_ref, image_ref, back_ref, right_ref, vec_ref
):
    pair = on_pair()

    def set_rows(k, points, depth):
        features, columns = points
        at = slice(k * 128, (k + 1) * 128)
        left_ref[at, :depth] = operand(features, True, depth).T
        rows_ref[k] = columns
        flat_ref[:, at] = jnp.concatenate(halves(columns), axis=0)

    def multiply(depth, rows, prepare, ranges):
        for r in range(2 * HALF // rows):
            strip = slice(rows * r, rows * (r + 1))
            ahead = strip.stop + AHEAD
            for k in range((strip.start + AHEAD if r else 0) // 128, min(ahead, 2 * HALF) // 128):
                prepare(k)
            at, back_from = ranges(strip)
            total = block(
                depth, left_ref, flat_ref, right_ref, vec_ref, back_ref,
                strip, at, back_from, r == 0,
            )
            for n in range(rows // 128):
                both = total[128 * n : 128 * (n + 1)].T
                image_ref[rows // 128 * r + n] = both[:32] + both[32:]

    @pl.when(pair)
    def _():
        for n in range(TILES // 2):
            at = slice(128 * n, 128 * n + 128)
            set_columns(right_ref, vec_ref, at, half_points_of(own_ref, n, 16), DEPTH)
        multiply(
            DEPTH,
            PAIR_ROWS,
            lambda k: set_rows(k, points_of(own_ref, k, 0), DEPTH),
            lambda strip: (slice(0, HALF), 0),
        )

    @pl.when(jnp.logical_not(pair))
    def _():
        for k in range(TILES):
            points = points_of(own_ref, k, 8)
            set_rows(k, points, SHALLOW)
            set_columns(right_ref, vec_ref, slice(128 * k, 128 * k + 128), points, SHALLOW)
        multiply(
            SHALLOW, ROWS, lambda k: None, lambda strip: (slice(strip.start, 2 * HALF), strip.stop)
        )
        for k in range(ROWS // 128, TILES):
            at = slice(128 * k, 128 * (k + 1))
            image_ref[k] = image_ref[k] + (back_ref[:32, at] + back_ref[32:, at])


def far_kernel(
    other_ref, left_ref, rows_ref, flat_ref, image_ref, back_in_ref,
    whole_ref, low_ref, far_ref, right_ref, vec_ref, back_ref,
):
    pair = on_pair()
    core = lax.axis_index("c")
    lane = lax.broadcasted_iota(jnp.int32, (8, 128), 1)

    def multiply(depth, step, columns_of, both_times, square_times, beside=None):
        product = jnp.zeros((32, 128), F32)
        square = jnp.zeros((32, 128), F32)
        for r in range(2 * HALF // step):
            strip = slice(step * r, step * (r + 1))
            at, first = columns_of(strip)
            if beside is not None:
                beside(r, 2 * HALF // step)
            total = block(
                depth, left_ref, flat_ref, right_ref, vec_ref, back_ref,
                strip, at, at.start, first,
            )
            for n in range(step // 128):
                k = step // 128 * r + n
                both = total[128 * n : 128 * (n + 1)].T
                cross = both[:32] + both[32:]
                rows = rows_ref[k]
                product = product + rows * (both_times * image_ref[k] + 2.0 * cross)
                if square_times:
                    square = square + rows * rows
                give_whole(whole_ref, k, image_ref[k] + cross)
        here = jnp.zeros((8, 128), F32)
        for n, x in enumerate((product, square)):
            x = jnp.sum(x, axis=1, keepdims=True)
            for m in range(4):
                to = 64 + 4 * (m // 2) + 2 * n + m % 2
                here = jnp.where(lane == to, x[8 * m : 8 * m + 8], here)
        far_ref[PEERS] = here

    def give_whole(ref, k, image):
        for xh in range(2):
            top, low = image[16 * xh : 16 * xh + 8], image[16 * xh + 8 : 16 * xh + 16]
            for chip in range(2):
                at = slice(64 * chip, 64 * (chip + 1))
                ref[CHIPS * xh + 2 * k + chip] = jnp.concatenate([top[:, at], low[:, at]], axis=1)

    @pl.when(pair)
    def _():
        for n in range(TILES // 2):
            at = slice(128 * n, 128 * n + 128)
            set_columns(right_ref, vec_ref, at, half_points_of(other_ref, n, 8), DEPTH)
        blank = jnp.zeros((8, 64), F32)

        def give_part(given, ref, k):
            at = slice(k * 128, (k + 1) * 128)
            image = given[:32, at] + given[32:, at]
            for xh in range(2):
                top, low = image[16 * xh : 16 * xh + 8], image[16 * xh + 8 : 16 * xh + 16]
                for j in range(4):
                    at = slice(32 * j, 32 * j + 32)
                    ref[CHIPS * xh + 4 * k + j] = jnp.concatenate(
                        [top[:, at], low[:, at], blank], axis=1
                    )

        def beside(r, steps):
            for k in range(r * (TILES // 2) // steps, (r + 1) * (TILES // 2) // steps):
                give_part(back_in_ref, low_ref, k)

        multiply(DEPTH, PAIR_ROWS, lambda strip: (slice(0, HALF), strip.start == 0), 2.0, 0, beside)
        for k in range(TILES // 2):
            give_part(back_ref, far_ref, k)

    @pl.when(jnp.logical_not(pair))
    def _():
        def place(k):
            half = (k // (TILES // 2) + core) % 2
            return pl.ds(pl.multiple_of(half * HALF + k % (TILES // 2) * 128, 128), 128)

        for k in range(TILES):
            set_columns(right_ref, vec_ref, place(k), points_of(other_ref, k, 0), SHALLOW)

        def columns_of(strip):
            start = strip.start // HALF * HALF
            return slice(start, start + HALF), strip.start == start

        multiply(SHALLOW, ROWS, columns_of, 1.0, 1)
        low_ref[...] = jnp.zeros_like(low_ref)
        for k in range(TILES):
            both = back_ref[:, place(k)]
            give_whole(far_ref, k, both[:32] + both[32:])


def join_kernel(whole_ref, low_ref, far_ref, near_ref, scale_ref, noise_ref, out_ref):
    pair = on_pair()
    lane = lax.broadcasted_iota(jnp.int32, (8, 128), 1)
    near = near_ref[:PEERS]
    sums = jnp.where(
        lane < 72,
        far_ref[PEERS] + near_ref[PEERS],
        jnp.where(lane < 100, scale_ref[0], noise_ref[0]),
    )
    out_ref[:, :8] = whole_ref[...] + jnp.where(pair, 0.0, near)
    out_ref[:, 8:] = low_ref[...] + jnp.where(pair, near, 0.0) + sums


def finish_kernel(got_ref, rhs_ref, sol_ref, res_ref):
    pair = got_ref[0, 8:]
    scale, noise = pair[0:1, 72:73], pair[0:1, 100:101]
    whole = [None] * GROUPS
    part = [None] * (2 * GROUPS)
    sums = got_ref[len(PAIRS), 8:]

    def plus(x, y):
        return y if x is None else x + y

    for k, (a, b, t) in enumerate(PAIRS):
        low = got_ref[k, 8:]
        whole[a] = plus(whole[a], got_ref[k, :8])
        part[2 * b + t] = plus(part[2 * b + t], low)
        sums = sums + low
    for a in range(GROUPS):
        whole[a] = plus(whole[a], got_ref[len(PAIRS) + a, :8])
        if a:
            sums = sums + got_ref[len(PAIRS) + a, 8:]
    mine = jnp.where(lax.axis_index("xh") == 0, sums[:, 64:68], sums[:, 68:72])
    product = jnp.concatenate([mine[:, 0:1], mine[:, 1:2]], axis=0)
    square = jnp.concatenate([mine[:, 2:3], mine[:, 3:4]], axis=0)
    step = square / (scale * product + noise * square)
    image = jnp.concatenate(
        [
            jnp.concatenate(
                [
                    x[:, 64 * m + 32 * h : 64 * m + 32 * h + 32]
                    for h in range(2)
                    for x in whole
                ],
                axis=1,
            )
            for m in range(2)
        ],
        axis=0,
    )
    blank = jnp.zeros((8, 16), F32)
    image = image + jnp.concatenate(
        [
            jnp.concatenate(
                [
                    blank if x is None else x[:, 32 * m + 16 * h : 32 * m + 16 * h + 16]
                    for h in range(2)
                    for x in part
                ],
                axis=1,
            )
            for m in range(2)
        ],
        axis=0,
    )
    direction = rhs_ref[...]
    sol_ref[...] = step * direction
    res_ref[...] = direction - step * (scale * image + noise * direction)


def on_device(encodings, first_weight, second_weight, inv_scale, outputscale, noise, rhs):
    hbm, vmem = pl.BlockSpec(memory_space=pltpu.HBM), pl.BlockSpec(memory_space=pltpu.VMEM)
    swap = [(0, 1), (1, 0)]
    sent = pl.pallas_call(
        pack_kernel,
        out_shape=pltpu.VMEM((PEERS, 24, 128), F32),
        in_specs=[hbm] * 5,
        scratch_shapes=[
            pltpu.VMEM(encodings.shape, BF16),
            pltpu.VMEM(first_weight.shape, BF16),
            pltpu.VMEM(second_weight.shape[::-1], BF16),
            pltpu.VMEM((1, inv_scale.size), F32),
            pltpu.VMEM(rhs.shape, F32),
            pltpu.VMEM((GROUPS, 16, 128), F32),
            pltpu.VMEM((2 * GROUPS, 8, 128), F32),
            pltpu.SemaphoreType.DMA((2 * STEPS,)),
            pltpu.SemaphoreType.DMA((3,)),
        ],
        name="features",
    )(encodings, first_weight, second_weight.T, inv_scale.reshape(1, -1), rhs)
    own = lax.all_to_all(sent, ("xh", "g"), 0, 0, tiled=True)
    other = lax.ppermute(own[:, 8:], "c", swap)
    cost = pl.CostEstimate(flops=4 << 30, bytes_accessed=1 << 20, transcendentals=1 << 21)
    *rows, back = pl.pallas_call(
        near_kernel,
        out_shape=(
            jax.ShapeDtypeStruct((2 * HALF, DEPTH), BF16),
            jax.ShapeDtypeStruct((TILES, 32, 128), F32),
            jax.ShapeDtypeStruct((64, 2 * HALF), BF16),
            jax.ShapeDtypeStruct((TILES, 32, 128), F32),
            jax.ShapeDtypeStruct((64, 2 * HALF), F32),
        ),
        scratch_shapes=[
            pltpu.VMEM((DEPTH, 2 * HALF), BF16),
            pltpu.VMEM((2 * HALF, 64), BF16),
        ],
        compiler_params=pltpu.CompilerParams(vmem_limit_bytes=24 << 20),
        cost_estimate=cost,
        name="own_columns",
    )(own)
    whole, low, far = pl.pallas_call(
        far_kernel,
        out_shape=tuple(jax.ShapeDtypeStruct((n, 8, 128), F32) for n in (PEERS, PEERS, PEERS + 1)),
        scratch_shapes=[
            pltpu.VMEM((DEPTH, 2 * HALF), BF16),
            pltpu.VMEM((2 * HALF, 64), BF16),
            pltpu.VMEM((64, 2 * HALF), F32),
        ],
        compiler_params=pltpu.CompilerParams(vmem_limit_bytes=24 << 20),
        cost_estimate=cost,
        name="other_columns",
    )(other, *rows, back)
    near = lax.ppermute(far, "c", swap)
    smem = pl.BlockSpec(memory_space=pltpu.SMEM)
    partial = pl.pallas_call(
        join_kernel,
        out_shape=jax.ShapeDtypeStruct((PEERS, 16, 128), F32),
        in_specs=[vmem] * 4 + [smem] * 2,
        compiler_params=pltpu.CompilerParams(vmem_limit_bytes=8 << 20),
        name="join",
    )(whole, low, far, near, outputscale, noise)
    got = lax.all_to_all(partial, ("xh", "g"), 0, 0, tiled=True)
    return pl.pallas_call(
        finish_kernel,
        out_shape=(jax.ShapeDtypeStruct(rhs.shape, F32),) * 2,
        in_specs=[vmem] * 2,
        compiler_params=pltpu.CompilerParams(vmem_limit_bytes=8 << 20),
        name="update",
    )(got, rhs)


def solution(mesh):
    split = Mesh(mesh.devices.reshape(CHIPS, 2, 2), ("g", "c", "xh"))
    vectors = P("xh", ("g", "c"))
    return jax.shard_map(
        on_device,
        mesh=split,
        in_specs=(P(("g", "c", "xh"), None), P(), P(), P(), P(), P(), vectors),
        out_specs=(vectors, vectors),
        check_vma=False,
    )
```

```python
import jax
import jax.numpy as jnp
from jax import lax
from jax.experimental import pallas as pl
from jax.experimental.pallas import tpu as pltpu
from jax.sharding import Mesh
from jax.sharding import PartitionSpec as P

F32, BF16 = jnp.float32, jnp.bfloat16
ROOT_LOG2E = 1.2011224087864498
CHIPS = 32
PEERS = 64
GROUPS = 8
WIDTH = 32
DEPTH = 256
SHALLOW = 144
STEPS = 4
ROWS = 256
PAIR_ROWS = 512
AHEAD = 0
PAIRS = [(a, b, t) for a in range(GROUPS) for b in range(a + 1, GROUPS) for t in range(2)]
TILES = CHIPS // 2
HALF = TILES * 128 // 2


def halves(x):
    high = x.astype(BF16)
    return high, (x - high.astype(F32)).astype(BF16)


def pack_kernel(
    enc_hbm, w1_hbm, w2_hbm, inv_hbm, rhs_hbm, out_ref,
    enc_ref, w1_ref, w2_ref, inv_ref, rhs_ref, set_ref, part_ref, big_sem, sem,
):
    small = [
        pltpu.make_async_copy(src, dst, sem.at[n])
        for n, (src, dst) in enumerate(
            ((w2_hbm, w2_ref), (inv_hbm, inv_ref), (rhs_hbm, rhs_ref))
        )
    ]
    depth = enc_hbm.shape[1] // STEPS
    big = []
    for n in range(STEPS):
        at = pl.ds(n * depth, depth)
        big.append(
            (
                pltpu.make_async_copy(enc_hbm.at[:, at], enc_ref.at[:, at], big_sem.at[2 * n]),
                pltpu.make_async_copy(w1_hbm.at[at], w1_ref.at[at], big_sem.at[2 * n + 1]),
            )
        )
    for pair in big:
        for copy in pair:
            copy.start()
    for copy in small:
        copy.start()
    hidden = jnp.zeros((enc_hbm.shape[0], w1_hbm.shape[1]), F32)
    for n in range(STEPS):
        at = slice(n * depth, (n + 1) * depth)
        for copy in big[n]:
            copy.wait()
        hidden = hidden + jnp.dot(enc_ref[:, at], w1_ref[at], preferred_element_type=F32)
    hidden = jnp.maximum(hidden, 0.0).astype(BF16)
    for copy in small:
        copy.wait()
    features = lax.dot_general(
        w2_ref[...], hidden, (((1,), (1,)), ((), ())), preferred_element_type=F32
    )
    n = features.shape[0]
    diagonal = lax.broadcasted_iota(jnp.int32, (n, n), 0) == lax.broadcasted_iota(
        jnp.int32, (n, n), 1
    )
    inv = jnp.sum(
        jnp.where(diagonal, jnp.broadcast_to(inv_ref[...], (n, n)), 0.0), axis=1, keepdims=True
    )
    features = features * inv * ROOT_LOG2E
    late = rhs_ref.shape[1] // 2
    for a in range(GROUPS):
        lo = WIDTH * a
        at, after = slice(lo, lo + WIDTH), slice(late + lo, late + lo + WIDTH)
        set_ref[a] = jnp.concatenate(
            [features[:16, at], features[16:, at], rhs_ref[:, at], rhs_ref[:, after]], axis=1
        )
        for t in range(2):
            lo = WIDTH * a + 16 * t
            at, after = slice(lo, lo + 16), slice(late + lo, late + lo + 16)
            part_ref[2 * a + t] = jnp.concatenate(
                [features[8 * m : 8 * m + 8, at] for m in range(4)]
                + [rhs_ref[8 * m : 8 * m + 8, s] for m in range(2) for s in (at, after)],
                axis=1,
            )
    for k, (a, b, t) in enumerate(PAIRS):
        out_ref[k, :16] = set_ref[a]
        out_ref[k, 16:] = part_ref[2 * b + t]
    for a in range(GROUPS):
        out_ref[len(PAIRS) + a, :8] = jnp.zeros((8, 128), F32)
        out_ref[len(PAIRS) + a, 8:] = set_ref[a]


def points_of(ref, k, lo):
    a0, a1 = ref[2 * k, lo : lo + 16], ref[2 * k + 1, lo : lo + 16]
    b0, b1 = ref[CHIPS + 2 * k, lo : lo + 16], ref[CHIPS + 2 * k + 1, lo : lo + 16]
    four = (a0, b0, a1, b1)
    features = jnp.concatenate(
        [
            jnp.concatenate([x[:, :32] for x in four], axis=1),
            jnp.concatenate([x[:, 32:64] for x in four], axis=1),
        ],
        axis=0,
    )
    columns = jnp.concatenate(
        [
            jnp.concatenate([a0[:, 64:], a1[:, 64:]], axis=1),
            jnp.concatenate([b0[:, 64:], b1[:, 64:]], axis=1),
        ],
        axis=0,
    )
    return features, columns


def half_points_of(ref, k, lo):
    units = [[ref[CHIPS * xh + 4 * k + j, lo : lo + 8] for xh in range(2)] for j in range(4)]
    features = jnp.concatenate(
        [
            jnp.concatenate([u[:, 16 * m : 16 * m + 16] for pair in units for u in pair], axis=1)
            for m in range(4)
        ],
        axis=0,
    )
    columns = jnp.concatenate(
        [
            jnp.concatenate([pair[xh][:, s : s + 32] for pair in units], axis=1)
            for xh in range(2)
            for s in (64, 96)
        ],
        axis=0,
    )
    return features, columns


def operand(features, left, depth):
    y1, y2 = halves(features)
    kept = y1.astype(F32) + y2.astype(F32)
    norm = -0.5 * jnp.sum(kept * kept, axis=0, keepdims=True)
    n1 = norm.astype(BF16).astype(F32)
    n2 = (norm - n1).astype(BF16).astype(F32)
    n3 = norm - n1 - n2
    row = lax.broadcasted_iota(jnp.int32, (16, features.shape[1]), 0)
    own, other = (3, 0) if left else (0, 3)
    tail = jnp.where(
        row == own,
        n1,
        jnp.where(
            row == own + 1,
            n2,
            jnp.where(
                row == own + 2, n3, jnp.where((row >= other) & (row < other + 3), 1.0, 0.0)
            ),
        ),
    ).astype(BF16)
    parts = ([y1, y1, y2, y2] if left else [y1, y2, y1, y2]) + [tail]
    if depth > SHALLOW:
        parts.append(jnp.zeros((depth - SHALLOW, features.shape[1]), BF16))
    return jnp.concatenate(parts, axis=0)


def on_pair():
    return lax.axis_index("xh") * CHIPS + lax.axis_index("g") < len(PAIRS)


def set_columns(right_ref, vec_ref, at, points, depth):
    features, columns = points
    right_ref[:depth, at] = operand(features, False, depth)
    parts = jnp.concatenate(halves(columns), axis=0)
    if vec_ref.shape[0] == 64:
        vec_ref[:, at] = parts
    else:
        vec_ref[at, :] = parts.T


def block(depth, left_ref, flat_ref, right_ref, vec_ref, back_ref, strip, at, back_from, first):
    exponent = jnp.dot(
        left_ref[strip, :depth], right_ref[:depth, at], preferred_element_type=F32
    )
    tile = jnp.exp2(exponent).astype(BF16)
    if vec_ref.shape[0] == 64:
        total = lax.dot_general(
            vec_ref[:, at], tile, (((1,), (1,)), ((), ())), preferred_element_type=F32
        )
    else:
        total = jnp.dot(tile, vec_ref[at, :], preferred_element_type=F32).T
    if back_from < at.stop:
        to = slice(back_from, at.stop)
        back = jnp.dot(
            flat_ref[:, strip], tile[:, back_from - at.start :], preferred_element_type=F32
        )
        back_ref[:, to] = back if first else back_ref[:, to] + back
    return total


def near_kernel(
    own_ref, left_ref, rows_ref, flat_ref, image_ref, back_ref, right_ref, vec_ref, line_ref
):
    pair = on_pair()

    def set_rows(k, points, depth):
        features, columns = points
        at = slice(k * 128, (k + 1) * 128)
        left_ref[at, :depth] = operand(features, True, depth).T
        rows_ref[k] = columns
        flat_ref[:, at] = jnp.concatenate(halves(columns), axis=0)

    def multiply(vec_ref, depth, rows, prepare, ranges):
        for r in range(2 * HALF // rows):
            strip = slice(rows * r, rows * (r + 1))
            ahead = strip.stop + AHEAD
            for k in range((strip.start + AHEAD if r else 0) // 128, min(ahead, 2 * HALF) // 128):
                prepare(k)
            at, back_from = ranges(strip)
            total = block(
                depth, left_ref, flat_ref, right_ref, vec_ref, back_ref,
                strip, at, back_from, r == 0,
            )
            for n in range(rows // 128):
                both = total[:, 128 * n : 128 * (n + 1)]
                image_ref[rows // 128 * r + n] = both[:32] + both[32:]

    @pl.when(pair)
    def _():
        for n in range(TILES // 2):
            at = slice(128 * n, 128 * n + 128)
            set_columns(right_ref, line_ref, at, half_points_of(own_ref, n, 16), DEPTH)
        multiply(
            line_ref,
            DEPTH,
            ROWS,
            lambda k: set_rows(k, points_of(own_ref, k, 0), DEPTH),
            lambda strip: (slice(0, HALF), 0),
        )

    @pl.when(jnp.logical_not(pair))
    def _():
        for k in range(TILES):
            points = points_of(own_ref, k, 8)
            set_rows(k, points, SHALLOW)
            set_columns(right_ref, vec_ref, slice(128 * k, 128 * k + 128), points, SHALLOW)
        multiply(
            vec_ref, SHALLOW, ROWS, lambda k: None, lambda strip: (slice(strip.start, 2 * HALF), strip.stop)
        )
        for k in range(ROWS // 128, TILES):
            at = slice(128 * k, 128 * (k + 1))
            image_ref[k] = image_ref[k] + (back_ref[:32, at] + back_ref[32:, at])


def far_kernel(
    other_ref, left_ref, rows_ref, flat_ref, image_ref, back_in_ref,
    whole_ref, low_ref, far_ref, right_ref, vec_ref, line_ref, back_ref,
):
    pair = on_pair()
    core = lax.axis_index("c")
    lane = lax.broadcasted_iota(jnp.int32, (8, 128), 1)

    def multiply(vec_ref, depth, step, columns_of, both_times, square_times, beside=None):
        product = jnp.zeros((32, 128), F32)
        square = jnp.zeros((32, 128), F32)
        for r in range(2 * HALF // step):
            strip = slice(step * r, step * (r + 1))
            at, first = columns_of(strip)
            if beside is not None:
                beside(r, 2 * HALF // step)
            total = block(
                depth, left_ref, flat_ref, right_ref, vec_ref, back_ref,
                strip, at, at.start, first,
            )
            for n in range(step // 128):
                k = step // 128 * r + n
                both = total[:, 128 * n : 128 * (n + 1)]
                cross = both[:32] + both[32:]
                rows = rows_ref[k]
                product = product + rows * (both_times * image_ref[k] + 2.0 * cross)
                if square_times:
                    square = square + rows * rows
                give_whole(whole_ref, k, image_ref[k] + cross)
        here = jnp.zeros((8, 128), F32)
        for n, x in enumerate((product, square)):
            x = jnp.sum(x, axis=1, keepdims=True)
            for m in range(4):
                to = 64 + 4 * (m // 2) + 2 * n + m % 2
                here = jnp.where(lane == to, x[8 * m : 8 * m + 8], here)
        far_ref[PEERS] = here

    def give_whole(ref, k, image):
        for xh in range(2):
            top, low = image[16 * xh : 16 * xh + 8], image[16 * xh + 8 : 16 * xh + 16]
            for chip in range(2):
                at = slice(64 * chip, 64 * (chip + 1))
                ref[CHIPS * xh + 2 * k + chip] = jnp.concatenate([top[:, at], low[:, at]], axis=1)

    @pl.when(pair)
    def _():
        for n in range(TILES // 2):
            at = slice(128 * n, 128 * n + 128)
            set_columns(right_ref, line_ref, at, half_points_of(other_ref, n, 8), DEPTH)
        blank = jnp.zeros((8, 64), F32)

        def give_part(given, ref, k):
            at = slice(k * 128, (k + 1) * 128)
            image = given[:32, at] + given[32:, at]
            for xh in range(2):
                top, low = image[16 * xh : 16 * xh + 8], image[16 * xh + 8 : 16 * xh + 16]
                for j in range(4):
                    at = slice(32 * j, 32 * j + 32)
                    ref[CHIPS * xh + 4 * k + j] = jnp.concatenate(
                        [top[:, at], low[:, at], blank], axis=1
                    )

        def beside(r, steps):
            for k in range(r * (TILES // 2) // steps, (r + 1) * (TILES // 2) // steps):
                give_part(back_in_ref, low_ref, k)

        multiply(line_ref, DEPTH, PAIR_ROWS, lambda strip: (slice(0, HALF), strip.start == 0), 2.0, 0, beside)
        for k in range(TILES // 2):
            give_part(back_ref, far_ref, k)

    @pl.when(jnp.logical_not(pair))
    def _():
        def place(k):
            half = (k // (TILES // 2) + core) % 2
            return pl.ds(pl.multiple_of(half * HALF + k % (TILES // 2) * 128, 128), 128)

        for k in range(TILES):
            set_columns(right_ref, vec_ref, place(k), points_of(other_ref, k, 0), SHALLOW)

        def columns_of(strip):
            start = strip.start // HALF * HALF
            return slice(start, start + HALF), strip.start == start

        multiply(vec_ref, SHALLOW, ROWS, columns_of, 1.0, 1)
        low_ref[...] = jnp.zeros_like(low_ref)
        for k in range(TILES):
            both = back_ref[:, place(k)]
            give_whole(far_ref, k, both[:32] + both[32:])


def join_kernel(whole_ref, low_ref, far_ref, near_ref, scale_ref, noise_ref, out_ref):
    pair = on_pair()
    lane = lax.broadcasted_iota(jnp.int32, (8, 128), 1)
    near = near_ref[:PEERS]
    sums = jnp.where(
        lane < 72,
        far_ref[PEERS] + near_ref[PEERS],
        jnp.where(lane < 100, scale_ref[0], noise_ref[0]),
    )
    out_ref[:, :8] = whole_ref[...] + jnp.where(pair, 0.0, near)
    out_ref[:, 8:] = low_ref[...] + jnp.where(pair, near, 0.0) + sums


def finish_kernel(got_ref, rhs_ref, sol_ref, res_ref):
    pair = got_ref[0, 8:]
    scale, noise = pair[0:1, 72:73], pair[0:1, 100:101]
    whole = [None] * GROUPS
    part = [None] * (2 * GROUPS)
    sums = got_ref[len(PAIRS), 8:]

    def plus(x, y):
        return y if x is None else x + y

    for k, (a, b, t) in enumerate(PAIRS):
        low = got_ref[k, 8:]
        whole[a] = plus(whole[a], got_ref[k, :8])
        part[2 * b + t] = plus(part[2 * b + t], low)
        sums = sums + low
    for a in range(GROUPS):
        whole[a] = plus(whole[a], got_ref[len(PAIRS) + a, :8])
        if a:
            sums = sums + got_ref[len(PAIRS) + a, 8:]
    mine = jnp.where(lax.axis_index("xh") == 0, sums[:, 64:68], sums[:, 68:72])
    product = jnp.concatenate([mine[:, 0:1], mine[:, 1:2]], axis=0)
    square = jnp.concatenate([mine[:, 2:3], mine[:, 3:4]], axis=0)
    step = square / (scale * product + noise * square)
    image = jnp.concatenate(
        [
            jnp.concatenate(
                [
                    x[:, 64 * m + 32 * h : 64 * m + 32 * h + 32]
                    for h in range(2)
                    for x in whole
                ],
                axis=1,
            )
            for m in range(2)
        ],
        axis=0,
    )
    blank = jnp.zeros((8, 16), F32)
    image = image + jnp.concatenate(
        [
            jnp.concatenate(
                [
                    blank if x is None else x[:, 32 * m + 16 * h : 32 * m + 16 * h + 16]
                    for h in range(2)
                    for x in part
                ],
                axis=1,
            )
            for m in range(2)
        ],
        axis=0,
    )
    direction = rhs_ref[...]
    sol_ref[...] = step * direction
    res_ref[...] = direction - step * (scale * image + noise * direction)


def on_device(encodings, first_weight, second_weight, inv_scale, outputscale, noise, rhs):
    hbm, vmem = pl.BlockSpec(memory_space=pltpu.HBM), pl.BlockSpec(memory_space=pltpu.VMEM)
    swap = [(0, 1), (1, 0)]
    sent = pl.pallas_call(
        pack_kernel,
        out_shape=pltpu.VMEM((PEERS, 24, 128), F32),
        in_specs=[hbm] * 5,
        scratch_shapes=[
            pltpu.VMEM(encodings.shape, BF16),
            pltpu.VMEM(first_weight.shape, BF16),
            pltpu.VMEM(second_weight.shape[::-1], BF16),
            pltpu.VMEM((1, inv_scale.size), F32),
            pltpu.VMEM(rhs.shape, F32),
            pltpu.VMEM((GROUPS, 16, 128), F32),
            pltpu.VMEM((2 * GROUPS, 8, 128), F32),
            pltpu.SemaphoreType.DMA((2 * STEPS,)),
            pltpu.SemaphoreType.DMA((3,)),
        ],
        name="features",
    )(encodings, first_weight, second_weight.T, inv_scale.reshape(1, -1), rhs)
    own = lax.all_to_all(sent, ("xh", "g"), 0, 0, tiled=True)
    other = lax.ppermute(own[:, 8:], "c", swap)
    cost = pl.CostEstimate(flops=4 << 30, bytes_accessed=1 << 20, transcendentals=1 << 21)
    *rows, back = pl.pallas_call(
        near_kernel,
        out_shape=(
            jax.ShapeDtypeStruct((2 * HALF, DEPTH), BF16),
            jax.ShapeDtypeStruct((TILES, 32, 128), F32),
            jax.ShapeDtypeStruct((64, 2 * HALF), BF16),
            jax.ShapeDtypeStruct((TILES, 32, 128), F32),
            jax.ShapeDtypeStruct((64, 2 * HALF), F32),
        ),
        scratch_shapes=[
            pltpu.VMEM((DEPTH, 2 * HALF), BF16),
            pltpu.VMEM((2 * HALF, 64), BF16),
            pltpu.VMEM((64, HALF), BF16),
        ],
        compiler_params=pltpu.CompilerParams(vmem_limit_bytes=24 << 20),
        cost_estimate=cost,
        name="own_columns",
    )(own)
    whole, low, far = pl.pallas_call(
        far_kernel,
        out_shape=tuple(jax.ShapeDtypeStruct((n, 8, 128), F32) for n in (PEERS, PEERS, PEERS + 1)),
        scratch_shapes=[
            pltpu.VMEM((DEPTH, 2 * HALF), BF16),
            pltpu.VMEM((2 * HALF, 64), BF16),
            pltpu.VMEM((64, HALF), BF16),
            pltpu.VMEM((64, 2 * HALF), F32),
        ],
        compiler_params=pltpu.CompilerParams(vmem_limit_bytes=24 << 20),
        cost_estimate=cost,
        name="other_columns",
    )(other, *rows, back)
    near = lax.ppermute(far, "c", swap)
    smem = pl.BlockSpec(memory_space=pltpu.SMEM)
    partial = pl.pallas_call(
        join_kernel,
        out_shape=jax.ShapeDtypeStruct((PEERS, 16, 128), F32),
        in_specs=[vmem] * 4 + [smem] * 2,
        compiler_params=pltpu.CompilerParams(vmem_limit_bytes=8 << 20),
        name="join",
    )(whole, low, far, near, outputscale, noise)
    got = lax.all_to_all(partial, ("xh", "g"), 0, 0, tiled=True)
    return pl.pallas_call(
        finish_kernel,
        out_shape=(jax.ShapeDtypeStruct(rhs.shape, F32),) * 2,
        in_specs=[vmem] * 2,
        compiler_params=pltpu.CompilerParams(vmem_limit_bytes=8 << 20),
        name="update",
    )(got, rhs)


def solution(mesh):
    split = Mesh(mesh.devices.reshape(CHIPS, 2, 2), ("g", "c", "xh"))
    vectors = P("xh", ("g", "c"))
    return jax.shard_map(
        on_device,
        mesh=split,
        in_specs=(P(("g", "c", "xh"), None), P(), P(), P(), P(), P(), vectors),
        out_specs=(vectors, vectors),
        check_vma=False,
    )
```

```python
import jax
import jax.numpy as jnp
from jax import lax
from jax.experimental import pallas as pl
from jax.experimental.pallas import tpu as pltpu
from jax.sharding import Mesh
from jax.sharding import PartitionSpec as P

F32, BF16 = jnp.float32, jnp.bfloat16
ROOT_LOG2E = 1.2011224087864498
CHIPS = 32
PEERS = 64
GROUPS = 8
WIDTH = 32
DEPTH = 256
SHALLOW = 144
STEPS = 4
FEW_ROWS = 256
ROWS = 512
AHEAD = 0
PAIRS = [(a, b, t) for a in range(GROUPS) for b in range(a + 1, GROUPS) for t in range(2)]
TILES = CHIPS // 2
HALF = TILES * 128 // 2


def halves(x):
    high = x.astype(BF16)
    return high, (x - high.astype(F32)).astype(BF16)


def pack_kernel(
    enc_hbm, w1_hbm, w2_hbm, inv_hbm, rhs_hbm, out_ref,
    enc_ref, w1_ref, w2_ref, inv_ref, rhs_ref, set_ref, part_ref, big_sem, sem,
):
    small = [
        pltpu.make_async_copy(src, dst, sem.at[n])
        for n, (src, dst) in enumerate(
            ((w2_hbm, w2_ref), (inv_hbm, inv_ref), (rhs_hbm, rhs_ref))
        )
    ]
    depth = enc_hbm.shape[1] // STEPS
    big = []
    for n in range(STEPS):
        at = pl.ds(n * depth, depth)
        big.append(
            (
                pltpu.make_async_copy(enc_hbm.at[:, at], enc_ref.at[:, at], big_sem.at[2 * n]),
                pltpu.make_async_copy(w1_hbm.at[at], w1_ref.at[at], big_sem.at[2 * n + 1]),
            )
        )
    for pair in big:
        for copy in pair:
            copy.start()
    for copy in small:
        copy.start()
    hidden = jnp.zeros((enc_hbm.shape[0], w1_hbm.shape[1]), F32)
    for n in range(STEPS):
        at = slice(n * depth, (n + 1) * depth)
        for copy in big[n]:
            copy.wait()
        hidden = hidden + jnp.dot(enc_ref[:, at], w1_ref[at], preferred_element_type=F32)
    hidden = jnp.maximum(hidden, 0.0).astype(BF16)
    for copy in small:
        copy.wait()
    features = lax.dot_general(
        w2_ref[...], hidden, (((1,), (1,)), ((), ())), preferred_element_type=F32
    )
    n = features.shape[0]
    diagonal = lax.broadcasted_iota(jnp.int32, (n, n), 0) == lax.broadcasted_iota(
        jnp.int32, (n, n), 1
    )
    inv = jnp.sum(
        jnp.where(diagonal, jnp.broadcast_to(inv_ref[...], (n, n)), 0.0), axis=1, keepdims=True
    )
    features = features * inv * ROOT_LOG2E
    late = rhs_ref.shape[1] // 2
    for a in range(GROUPS):
        lo = WIDTH * a
        at, after = slice(lo, lo + WIDTH), slice(late + lo, late + lo + WIDTH)
        set_ref[a] = jnp.concatenate(
            [features[:16, at], features[16:, at], rhs_ref[:, at], rhs_ref[:, after]], axis=1
        )
        for t in range(2):
            lo = WIDTH * a + 16 * t
            at, after = slice(lo, lo + 16), slice(late + lo, late + lo + 16)
            part_ref[2 * a + t] = jnp.concatenate(
                [features[8 * m : 8 * m + 8, at] for m in range(4)]
                + [rhs_ref[8 * m : 8 * m + 8, s] for m in range(2) for s in (at, after)],
                axis=1,
            )
    for k, (a, b, t) in enumerate(PAIRS):
        out_ref[k, :16] = set_ref[a]
        out_ref[k, 16:] = part_ref[2 * b + t]
    for a in range(GROUPS):
        out_ref[len(PAIRS) + a, :8] = jnp.zeros((8, 128), F32)
        out_ref[len(PAIRS) + a, 8:] = set_ref[a]


def points_of(ref, k, lo):
    a0, a1 = ref[2 * k, lo : lo + 16], ref[2 * k + 1, lo : lo + 16]
    b0, b1 = ref[CHIPS + 2 * k, lo : lo + 16], ref[CHIPS + 2 * k + 1, lo : lo + 16]
    four = (a0, b0, a1, b1)
    features = jnp.concatenate(
        [
            jnp.concatenate([x[:, :32] for x in four], axis=1),
            jnp.concatenate([x[:, 32:64] for x in four], axis=1),
        ],
        axis=0,
    )
    columns = jnp.concatenate(
        [
            jnp.concatenate([a0[:, 64:], a1[:, 64:]], axis=1),
            jnp.concatenate([b0[:, 64:], b1[:, 64:]], axis=1),
        ],
        axis=0,
    )
    return features, columns


def half_points_of(ref, k, lo):
    units = [[ref[CHIPS * xh + 4 * k + j, lo : lo + 8] for xh in range(2)] for j in range(4)]
    features = jnp.concatenate(
        [
            jnp.concatenate([u[:, 16 * m : 16 * m + 16] for pair in units for u in pair], axis=1)
            for m in range(4)
        ],
        axis=0,
    )
    columns = jnp.concatenate(
        [
            jnp.concatenate([pair[xh][:, s : s + 32] for pair in units], axis=1)
            for xh in range(2)
            for s in (64, 96)
        ],
        axis=0,
    )
    return features, columns


def operand(features, left, depth):
    y1, y2 = halves(features)
    kept = y1.astype(F32) + y2.astype(F32)
    norm = -0.5 * jnp.sum(kept * kept, axis=0, keepdims=True)
    n1 = norm.astype(BF16).astype(F32)
    n2 = (norm - n1).astype(BF16).astype(F32)
    n3 = norm - n1 - n2
    row = lax.broadcasted_iota(jnp.int32, (16, features.shape[1]), 0)
    own, other = (3, 0) if left else (0, 3)
    tail = jnp.where(
        row == own,
        n1,
        jnp.where(
            row == own + 1,
            n2,
            jnp.where(
                row == own + 2, n3, jnp.where((row >= other) & (row < other + 3), 1.0, 0.0)
            ),
        ),
    ).astype(BF16)
    parts = ([y1, y1, y2, y2] if left else [y1, y2, y1, y2]) + [tail]
    if depth > SHALLOW:
        parts.append(jnp.zeros((depth - SHALLOW, features.shape[1]), BF16))
    return jnp.concatenate(parts, axis=0)


def on_pair():
    return lax.axis_index("xh") * CHIPS + lax.axis_index("g") < len(PAIRS)


def set_columns(right_ref, line_ref, at, points, depth):
    features, columns = points
    right_ref[:depth, at] = operand(features, False, depth)
    line_ref[:, at] = jnp.concatenate(halves(columns), axis=0)


def block(depth, left_ref, flat_ref, right_ref, line_ref, back_ref, strip, at, back_from, first):
    exponent = jnp.dot(
        left_ref[strip, :depth], right_ref[:depth, at], preferred_element_type=F32
    )
    tile = jnp.exp2(exponent).astype(BF16)
    total = lax.dot_general(
        line_ref[:, at], tile, (((1,), (1,)), ((), ())), preferred_element_type=F32
    )
    if back_from < at.stop:
        to = slice(back_from, at.stop)
        back = jnp.dot(
            flat_ref[:, strip], tile[:, back_from - at.start :], preferred_element_type=F32
        )
        back_ref[:, to] = back if first else back_ref[:, to] + back
    return total


def near_kernel(
    own_ref, left_ref, rows_ref, flat_ref, image_ref, back_ref, right_ref, line_ref
):
    pair = on_pair()

    def set_rows(k, points, depth):
        features, columns = points
        at = slice(k * 128, (k + 1) * 128)
        left_ref[at, :depth] = operand(features, True, depth).T
        rows_ref[k] = columns
        flat_ref[:, at] = jnp.concatenate(halves(columns), axis=0)

    def multiply(line_ref, depth, rows, prepare, ranges):
        for r in range(2 * HALF // rows):
            strip = slice(rows * r, rows * (r + 1))
            ahead = strip.stop + AHEAD
            for k in range((strip.start + AHEAD if r else 0) // 128, min(ahead, 2 * HALF) // 128):
                prepare(k)
            at, back_from = ranges(strip)
            total = block(
                depth, left_ref, flat_ref, right_ref, line_ref, back_ref,
                strip, at, back_from, r == 0,
            )
            for n in range(rows // 128):
                both = total[:, 128 * n : 128 * (n + 1)]
                image_ref[rows // 128 * r + n] = both[:32] + both[32:]

    @pl.when(pair)
    def _():
        for n in range(TILES // 2):
            at = slice(128 * n, 128 * n + 128)
            set_columns(right_ref, line_ref, at, half_points_of(own_ref, n, 16), DEPTH)
        multiply(
            line_ref,
            DEPTH,
            FEW_ROWS,
            lambda k: set_rows(k, points_of(own_ref, k, 0), DEPTH),
            lambda strip: (slice(0, HALF), 0),
        )

    @pl.when(jnp.logical_not(pair))
    def _():
        for k in range(TILES):
            points = points_of(own_ref, k, 8)
            set_rows(k, points, SHALLOW)
            right_ref[:SHALLOW, 128 * k : 128 * k + 128] = operand(points[0], False, SHALLOW)
        multiply(
            flat_ref, SHALLOW, ROWS, lambda k: None, lambda strip: (slice(strip.start, 2 * HALF), strip.stop)
        )
        for k in range(ROWS // 128, TILES):
            at = slice(128 * k, 128 * (k + 1))
            image_ref[k] = image_ref[k] + (back_ref[:32, at] + back_ref[32:, at])


def far_kernel(
    other_ref, left_ref, rows_ref, flat_ref, image_ref, back_in_ref,
    whole_ref, low_ref, far_ref, right_ref, line_ref, back_ref,
):
    pair = on_pair()
    core = lax.axis_index("c")
    lane = lax.broadcasted_iota(jnp.int32, (8, 128), 1)

    def multiply(depth, step, columns_of, both_times, square_times, beside=None):
        product = jnp.zeros((32, 128), F32)
        square = jnp.zeros((32, 128), F32)
        for r in range(2 * HALF // step):
            strip = slice(step * r, step * (r + 1))
            at, first = columns_of(strip)
            if beside is not None:
                beside(r, 2 * HALF // step)
            total = block(
                depth, left_ref, flat_ref, right_ref, line_ref, back_ref,
                strip, at, at.start, first,
            )
            for n in range(step // 128):
                k = step // 128 * r + n
                both = total[:, 128 * n : 128 * (n + 1)]
                cross = both[:32] + both[32:]
                rows = rows_ref[k]
                product = product + rows * (both_times * image_ref[k] + 2.0 * cross)
                if square_times:
                    square = square + rows * rows
                give_whole(whole_ref, k, image_ref[k] + cross)
        here = jnp.zeros((8, 128), F32)
        for n, x in enumerate((product, square)):
            x = jnp.sum(x, axis=1, keepdims=True)
            for m in range(4):
                to = 64 + 4 * (m // 2) + 2 * n + m % 2
                here = jnp.where(lane == to, x[8 * m : 8 * m + 8], here)
        far_ref[PEERS] = here

    def give_whole(ref, k, image):
        for xh in range(2):
            top, low = image[16 * xh : 16 * xh + 8], image[16 * xh + 8 : 16 * xh + 16]
            for chip in range(2):
                at = slice(64 * chip, 64 * (chip + 1))
                ref[CHIPS * xh + 2 * k + chip] = jnp.concatenate([top[:, at], low[:, at]], axis=1)

    @pl.when(pair)
    def _():
        for n in range(TILES // 2):
            at = slice(128 * n, 128 * n + 128)
            set_columns(right_ref, line_ref, at, half_points_of(other_ref, n, 8), DEPTH)
        blank = jnp.zeros((8, 64), F32)

        def give_part(given, ref, k):
            at = slice(k * 128, (k + 1) * 128)
            image = given[:32, at] + given[32:, at]
            for xh in range(2):
                top, low = image[16 * xh : 16 * xh + 8], image[16 * xh + 8 : 16 * xh + 16]
                for j in range(4):
                    at = slice(32 * j, 32 * j + 32)
                    ref[CHIPS * xh + 4 * k + j] = jnp.concatenate(
                        [top[:, at], low[:, at], blank], axis=1
                    )

        def beside(r, steps):
            for k in range(r * (TILES // 2) // steps, (r + 1) * (TILES // 2) // steps):
                give_part(back_in_ref, low_ref, k)

        multiply(DEPTH, ROWS, lambda strip: (slice(0, HALF), strip.start == 0), 2.0, 0, beside)
        for k in range(TILES // 2):
            give_part(back_ref, far_ref, k)

    @pl.when(jnp.logical_not(pair))
    def _():
        def place(k):
            half = (k // (TILES // 2) + core) % 2
            return pl.ds(pl.multiple_of(half * HALF + k % (TILES // 2) * 128, 128), 128)

        for k in range(TILES):
            set_columns(right_ref, line_ref, place(k), points_of(other_ref, k, 0), SHALLOW)

        def columns_of(strip):
            start = strip.start // HALF * HALF
            return slice(start, start + HALF), strip.start == start

        multiply(SHALLOW, ROWS, columns_of, 1.0, 1)
        low_ref[...] = jnp.zeros_like(low_ref)
        for k in range(TILES):
            both = back_ref[:, place(k)]
            give_whole(far_ref, k, both[:32] + both[32:])


def join_kernel(whole_ref, low_ref, far_ref, near_ref, scale_ref, noise_ref, out_ref):
    pair = on_pair()
    lane = lax.broadcasted_iota(jnp.int32, (8, 128), 1)
    near = near_ref[:PEERS]
    sums = jnp.where(
        lane < 72,
        far_ref[PEERS] + near_ref[PEERS],
        jnp.where(lane < 100, scale_ref[0], noise_ref[0]),
    )
    out_ref[:, :8] = whole_ref[...] + jnp.where(pair, 0.0, near)
    out_ref[:, 8:] = low_ref[...] + jnp.where(pair, near, 0.0) + sums


def finish_kernel(got_ref, rhs_ref, sol_ref, res_ref):
    pair = got_ref[0, 8:]
    scale, noise = pair[0:1, 72:73], pair[0:1, 100:101]
    whole = [None] * GROUPS
    part = [None] * (2 * GROUPS)
    sums = got_ref[len(PAIRS), 8:]

    def plus(x, y):
        return y if x is None else x + y

    for k, (a, b, t) in enumerate(PAIRS):
        low = got_ref[k, 8:]
        whole[a] = plus(whole[a], got_ref[k, :8])
        part[2 * b + t] = plus(part[2 * b + t], low)
        sums = sums + low
    for a in range(GROUPS):
        whole[a] = plus(whole[a], got_ref[len(PAIRS) + a, :8])
        if a:
            sums = sums + got_ref[len(PAIRS) + a, 8:]
    mine = jnp.where(lax.axis_index("xh") == 0, sums[:, 64:68], sums[:, 68:72])
    product = jnp.concatenate([mine[:, 0:1], mine[:, 1:2]], axis=0)
    square = jnp.concatenate([mine[:, 2:3], mine[:, 3:4]], axis=0)
    step = square / (scale * product + noise * square)
    image = jnp.concatenate(
        [
            jnp.concatenate(
                [
                    x[:, 64 * m + 32 * h : 64 * m + 32 * h + 32]
                    for h in range(2)
                    for x in whole
                ],
                axis=1,
            )
            for m in range(2)
        ],
        axis=0,
    )
    blank = jnp.zeros((8, 16), F32)
    image = image + jnp.concatenate(
        [
            jnp.concatenate(
                [
                    blank if x is None else x[:, 32 * m + 16 * h : 32 * m + 16 * h + 16]
                    for h in range(2)
                    for x in part
                ],
                axis=1,
            )
            for m in range(2)
        ],
        axis=0,
    )
    direction = rhs_ref[...]
    sol_ref[...] = step * direction
    res_ref[...] = direction - step * (scale * image + noise * direction)


def on_device(encodings, first_weight, second_weight, inv_scale, outputscale, noise, rhs):
    hbm, vmem = pl.BlockSpec(memory_space=pltpu.HBM), pl.BlockSpec(memory_space=pltpu.VMEM)
    swap = [(0, 1), (1, 0)]
    sent = pl.pallas_call(
        pack_kernel,
        out_shape=pltpu.VMEM((PEERS, 24, 128), F32),
        in_specs=[hbm] * 5,
        scratch_shapes=[
            pltpu.VMEM(encodings.shape, BF16),
            pltpu.VMEM(first_weight.shape, BF16),
            pltpu.VMEM(second_weight.shape[::-1], BF16),
            pltpu.VMEM((1, inv_scale.size), F32),
            pltpu.VMEM(rhs.shape, F32),
            pltpu.VMEM((GROUPS, 16, 128), F32),
            pltpu.VMEM((2 * GROUPS, 8, 128), F32),
            pltpu.SemaphoreType.DMA((2 * STEPS,)),
            pltpu.SemaphoreType.DMA((3,)),
        ],
        name="features",
    )(encodings, first_weight, second_weight.T, inv_scale.reshape(1, -1), rhs)
    own = lax.all_to_all(sent, ("xh", "g"), 0, 0, tiled=True)
    other = lax.ppermute(own[:, 8:], "c", swap)
    cost = pl.CostEstimate(flops=4 << 30, bytes_accessed=1 << 20, transcendentals=1 << 21)
    *rows, back = pl.pallas_call(
        near_kernel,
        out_shape=(
            jax.ShapeDtypeStruct((2 * HALF, DEPTH), BF16),
            jax.ShapeDtypeStruct((TILES, 32, 128), F32),
            jax.ShapeDtypeStruct((64, 2 * HALF), BF16),
            jax.ShapeDtypeStruct((TILES, 32, 128), F32),
            jax.ShapeDtypeStruct((64, 2 * HALF), F32),
        ),
        scratch_shapes=[
            pltpu.VMEM((DEPTH, 2 * HALF), BF16),
            pltpu.VMEM((64, 2 * HALF), BF16),
        ],
        compiler_params=pltpu.CompilerParams(vmem_limit_bytes=24 << 20),
        cost_estimate=cost,
        name="own_columns",
    )(own)
    whole, low, far = pl.pallas_call(
        far_kernel,
        out_shape=tuple(jax.ShapeDtypeStruct((n, 8, 128), F32) for n in (PEERS, PEERS, PEERS + 1)),
        scratch_shapes=[
            pltpu.VMEM((DEPTH, 2 * HALF), BF16),
            pltpu.VMEM((64, 2 * HALF), BF16),
            pltpu.VMEM((64, 2 * HALF), F32),
        ],
        compiler_params=pltpu.CompilerParams(vmem_limit_bytes=24 << 20),
        cost_estimate=cost,
        name="other_columns",
    )(other, *rows, back)
    near = lax.ppermute(far, "c", swap)
    smem = pl.BlockSpec(memory_space=pltpu.SMEM)
    partial = pl.pallas_call(
        join_kernel,
        out_shape=jax.ShapeDtypeStruct((PEERS, 16, 128), F32),
        in_specs=[vmem] * 4 + [smem] * 2,
        compiler_params=pltpu.CompilerParams(vmem_limit_bytes=8 << 20),
        name="join",
    )(whole, low, far, near, outputscale, noise)
    got = lax.all_to_all(partial, ("xh", "g"), 0, 0, tiled=True)
    return pl.pallas_call(
        finish_kernel,
        out_shape=(jax.ShapeDtypeStruct(rhs.shape, F32),) * 2,
        in_specs=[vmem] * 2,
        compiler_params=pltpu.CompilerParams(vmem_limit_bytes=8 << 20),
        name="update",
    )(got, rhs)


def solution(mesh):
    split = Mesh(mesh.devices.reshape(CHIPS, 2, 2), ("g", "c", "xh"))
    vectors = P("xh", ("g", "c"))
    return jax.shard_map(
        on_device,
        mesh=split,
        in_specs=(P(("g", "c", "xh"), None), P(), P(), P(), P(), P(), vectors),
        out_specs=(vectors, vectors),
        check_vma=False,
    )
```

```python
import jax
import jax.numpy as jnp
from jax import lax
from jax.experimental import pallas as pl
from jax.experimental.pallas import tpu as pltpu
from jax.sharding import Mesh
from jax.sharding import PartitionSpec as P

F32, BF16 = jnp.float32, jnp.bfloat16
ROOT_LOG2E = 1.2011224087864498
CHIPS = 32
PEERS = 64
GROUPS = 8
WIDTH = 32
DEPTH = 256
SHALLOW = 144
STEPS = 4
FEW_ROWS = 256
ROWS = 512
AHEAD = 0
PAIRS = [(a, b, t) for a in range(GROUPS) for b in range(a + 1, GROUPS) for t in range(2)]
TILES = CHIPS // 2
HALF = TILES * 128 // 2


def halves(x):
    high = x.astype(BF16)
    return high, (x - high.astype(F32)).astype(BF16)


def pack_kernel(
    enc_hbm, w1_hbm, w2_hbm, inv_hbm, rhs_hbm, out_ref,
    enc_ref, w1_ref, w2_ref, inv_ref, rhs_ref, set_ref, part_ref, big_sem, sem,
):
    small = [
        pltpu.make_async_copy(src, dst, sem.at[n])
        for n, (src, dst) in enumerate(
            ((w2_hbm, w2_ref), (inv_hbm, inv_ref), (rhs_hbm, rhs_ref))
        )
    ]
    depth = enc_hbm.shape[1] // STEPS
    big = []
    for n in range(STEPS):
        at = pl.ds(n * depth, depth)
        big.append(
            (
                pltpu.make_async_copy(enc_hbm.at[:, at], enc_ref.at[:, at], big_sem.at[2 * n]),
                pltpu.make_async_copy(w1_hbm.at[at], w1_ref.at[at], big_sem.at[2 * n + 1]),
            )
        )
    for pair in big:
        for copy in pair:
            copy.start()
    for copy in small:
        copy.start()
    hidden = jnp.zeros((enc_hbm.shape[0], w1_hbm.shape[1]), F32)
    for n in range(STEPS):
        at = slice(n * depth, (n + 1) * depth)
        for copy in big[n]:
            copy.wait()
        hidden = hidden + jnp.dot(enc_ref[:, at], w1_ref[at], preferred_element_type=F32)
    hidden = jnp.maximum(hidden, 0.0).astype(BF16)
    for copy in small:
        copy.wait()
    features = lax.dot_general(
        w2_ref[...], hidden, (((1,), (1,)), ((), ())), preferred_element_type=F32
    )
    n = features.shape[0]
    diagonal = lax.broadcasted_iota(jnp.int32, (n, n), 0) == lax.broadcasted_iota(
        jnp.int32, (n, n), 1
    )
    inv = jnp.sum(
        jnp.where(diagonal, jnp.broadcast_to(inv_ref[...], (n, n)), 0.0), axis=1, keepdims=True
    )
    features = features * inv * ROOT_LOG2E
    late = rhs_ref.shape[1] // 2
    for a in range(GROUPS):
        lo = WIDTH * a
        at, after = slice(lo, lo + WIDTH), slice(late + lo, late + lo + WIDTH)
        set_ref[a] = jnp.concatenate(
            [features[:16, at], features[16:, at], rhs_ref[:, at], rhs_ref[:, after]], axis=1
        )
        for t in range(2):
            lo = WIDTH * a + 16 * t
            at, after = slice(lo, lo + 16), slice(late + lo, late + lo + 16)
            part_ref[2 * a + t] = jnp.concatenate(
                [features[8 * m : 8 * m + 8, at] for m in range(4)]
                + [rhs_ref[8 * m : 8 * m + 8, s] for m in range(2) for s in (at, after)],
                axis=1,
            )
    for k, (a, b, t) in enumerate(PAIRS):
        out_ref[k, :16] = set_ref[a]
        out_ref[k, 16:] = part_ref[2 * b + t]
    for a in range(GROUPS):
        out_ref[len(PAIRS) + a, :8] = jnp.zeros((8, 128), F32)
        out_ref[len(PAIRS) + a, 8:] = set_ref[a]


def points_of(ref, k, lo):
    a0, a1 = ref[2 * k, lo : lo + 16], ref[2 * k + 1, lo : lo + 16]
    b0, b1 = ref[CHIPS + 2 * k, lo : lo + 16], ref[CHIPS + 2 * k + 1, lo : lo + 16]
    four = (a0, b0, a1, b1)
    features = jnp.concatenate(
        [
            jnp.concatenate([x[:, :32] for x in four], axis=1),
            jnp.concatenate([x[:, 32:64] for x in four], axis=1),
        ],
        axis=0,
    )
    columns = jnp.concatenate(
        [
            jnp.concatenate([a0[:, 64:], a1[:, 64:]], axis=1),
            jnp.concatenate([b0[:, 64:], b1[:, 64:]], axis=1),
        ],
        axis=0,
    )
    return features, columns


def half_points_of(ref, k, lo):
    units = [[ref[CHIPS * xh + 4 * k + j, lo : lo + 8] for xh in range(2)] for j in range(4)]
    features = jnp.concatenate(
        [
            jnp.concatenate([u[:, 16 * m : 16 * m + 16] for pair in units for u in pair], axis=1)
            for m in range(4)
        ],
        axis=0,
    )
    columns = jnp.concatenate(
        [
            jnp.concatenate([pair[xh][:, s : s + 32] for pair in units], axis=1)
            for xh in range(2)
            for s in (64, 96)
        ],
        axis=0,
    )
    return features, columns


def operand(features, left):
    y1, y2 = halves(features)
    kept = y1.astype(F32) + y2.astype(F32)
    norm = -0.5 * jnp.sum(kept * kept, axis=0, keepdims=True)
    n1 = norm.astype(BF16).astype(F32)
    n2 = (norm - n1).astype(BF16).astype(F32)
    n3 = norm - n1 - n2
    row = lax.broadcasted_iota(jnp.int32, (16, features.shape[1]), 0)
    own, other = (3, 0) if left else (0, 3)
    tail = jnp.where(
        row == own,
        n1,
        jnp.where(
            row == own + 1,
            n2,
            jnp.where(
                row == own + 2, n3, jnp.where((row >= other) & (row < other + 3), 1.0, 0.0)
            ),
        ),
    ).astype(BF16)
    parts = ([y1, y1, y2, y2] if left else [y1, y2, y1, y2]) + [tail]
    return jnp.concatenate(parts, axis=0)


def on_pair():
    return lax.axis_index("xh") * CHIPS + lax.axis_index("g") < len(PAIRS)


def set_columns(right_ref, line_ref, at, points, depth):
    features, columns = points
    right_ref[:SHALLOW, at] = operand(features, False)
    if depth > SHALLOW:
        right_ref[SHALLOW:, at] = jnp.zeros((depth - SHALLOW, 128), BF16)
    line_ref[:, at] = jnp.concatenate(halves(columns), axis=0)


def block(depth, left_ref, flat_ref, right_ref, line_ref, back_ref, strip, at, back_from, first):
    exponent = jnp.dot(
        left_ref[strip, :depth], right_ref[:depth, at], preferred_element_type=F32
    )
    tile = jnp.exp2(exponent).astype(BF16)
    total = lax.dot_general(
        line_ref[:, at], tile, (((1,), (1,)), ((), ())), preferred_element_type=F32
    )
    if back_from < at.stop:
        to = slice(back_from, at.stop)
        back = jnp.dot(
            flat_ref[:, strip], tile[:, back_from - at.start :], preferred_element_type=F32
        )
        back_ref[:, to] = back if first else back_ref[:, to] + back
    return total


def near_kernel(
    own_ref, left_ref, rows_ref, flat_ref, image_ref, back_ref, right_ref, line_ref
):
    pair = on_pair()

    def set_rows(k, points, depth):
        features, columns = points
        at = slice(k * 128, (k + 1) * 128)
        left_ref[at, :SHALLOW] = operand(features, True).T
        if depth > SHALLOW:
            left_ref[at, SHALLOW:] = jnp.zeros((128, depth - SHALLOW), BF16)
        rows_ref[k] = columns
        flat_ref[:, at] = jnp.concatenate(halves(columns), axis=0)

    def multiply(line_ref, depth, rows, prepare, ranges):
        for r in range(2 * HALF // rows):
            strip = slice(rows * r, rows * (r + 1))
            ahead = strip.stop + AHEAD
            for k in range((strip.start + AHEAD if r else 0) // 128, min(ahead, 2 * HALF) // 128):
                prepare(k)
            at, back_from = ranges(strip)
            total = block(
                depth, left_ref, flat_ref, right_ref, line_ref, back_ref,
                strip, at, back_from, r == 0,
            )
            for n in range(rows // 128):
                both = total[:, 128 * n : 128 * (n + 1)]
                image_ref[rows // 128 * r + n] = both[:32] + both[32:]

    @pl.when(pair)
    def _():
        for n in range(TILES // 2):
            at = slice(128 * n, 128 * n + 128)
            set_columns(right_ref, line_ref, at, half_points_of(own_ref, n, 16), DEPTH)
        multiply(
            line_ref,
            DEPTH,
            FEW_ROWS,
            lambda k: set_rows(k, points_of(own_ref, k, 0), DEPTH),
            lambda strip: (slice(0, HALF), 0),
        )

    @pl.when(jnp.logical_not(pair))
    def _():
        for k in range(TILES):
            points = points_of(own_ref, k, 8)
            set_rows(k, points, SHALLOW)
            right_ref[:SHALLOW, 128 * k : 128 * k + 128] = operand(points[0], False)
        multiply(
            flat_ref, SHALLOW, ROWS, lambda k: None, lambda strip: (slice(strip.start, 2 * HALF), strip.stop)
        )
        for k in range(ROWS // 128, TILES):
            at = slice(128 * k, 128 * (k + 1))
            image_ref[k] = image_ref[k] + (back_ref[:32, at] + back_ref[32:, at])


def far_kernel(
    other_ref, left_ref, rows_ref, flat_ref, image_ref, back_in_ref,
    whole_ref, low_ref, far_ref, right_ref, line_ref, back_ref,
):
    pair = on_pair()
    core = lax.axis_index("c")
    lane = lax.broadcasted_iota(jnp.int32, (8, 128), 1)

    def multiply(depth, step, columns_of, both_times, square_times, beside=None):
        product = jnp.zeros((32, 128), F32)
        square = jnp.zeros((32, 128), F32)
        for r in range(2 * HALF // step):
            strip = slice(step * r, step * (r + 1))
            at, first = columns_of(strip)
            if beside is not None:
                beside(r, 2 * HALF // step)
            total = block(
                depth, left_ref, flat_ref, right_ref, line_ref, back_ref,
                strip, at, at.start, first,
            )
            for n in range(step // 128):
                k = step // 128 * r + n
                both = total[:, 128 * n : 128 * (n + 1)]
                cross = both[:32] + both[32:]
                rows = rows_ref[k]
                product = product + rows * (both_times * image_ref[k] + 2.0 * cross)
                if square_times:
                    square = square + rows * rows
                give_whole(whole_ref, k, image_ref[k] + cross)
        here = jnp.zeros((8, 128), F32)
        for n, x in enumerate((product, square)):
            x = jnp.sum(x, axis=1, keepdims=True)
            for m in range(4):
                to = 64 + 4 * (m // 2) + 2 * n + m % 2
                here = jnp.where(lane == to, x[8 * m : 8 * m + 8], here)
        far_ref[PEERS] = here

    def give_whole(ref, k, image):
        for xh in range(2):
            top, low = image[16 * xh : 16 * xh + 8], image[16 * xh + 8 : 16 * xh + 16]
            for chip in range(2):
                at = slice(64 * chip, 64 * (chip + 1))
                ref[CHIPS * xh + 2 * k + chip] = jnp.concatenate([top[:, at], low[:, at]], axis=1)

    @pl.when(pair)
    def _():
        for n in range(TILES // 2):
            at = slice(128 * n, 128 * n + 128)
            set_columns(right_ref, line_ref, at, half_points_of(other_ref, n, 8), DEPTH)
        blank = jnp.zeros((8, 64), F32)

        def give_part(given, ref, k):
            at = slice(k * 128, (k + 1) * 128)
            image = given[:32, at] + given[32:, at]
            for xh in range(2):
                top, low = image[16 * xh : 16 * xh + 8], image[16 * xh + 8 : 16 * xh + 16]
                for j in range(4):
                    at = slice(32 * j, 32 * j + 32)
                    ref[CHIPS * xh + 4 * k + j] = jnp.concatenate(
                        [top[:, at], low[:, at], blank], axis=1
                    )

        def beside(r, steps):
            for k in range(r * (TILES // 2) // steps, (r + 1) * (TILES // 2) // steps):
                give_part(back_in_ref, low_ref, k)

        multiply(DEPTH, ROWS, lambda strip: (slice(0, HALF), strip.start == 0), 2.0, 0, beside)
        for k in range(TILES // 2):
            give_part(back_ref, far_ref, k)

    @pl.when(jnp.logical_not(pair))
    def _():
        def place(k):
            half = (k // (TILES // 2) + core) % 2
            return pl.ds(pl.multiple_of(half * HALF + k % (TILES // 2) * 128, 128), 128)

        for k in range(TILES):
            set_columns(right_ref, line_ref, place(k), points_of(other_ref, k, 0), SHALLOW)

        def columns_of(strip):
            start = strip.start // HALF * HALF
            return slice(start, start + HALF), strip.start == start

        multiply(SHALLOW, ROWS, columns_of, 1.0, 1)
        low_ref[...] = jnp.zeros_like(low_ref)
        for k in range(TILES):
            both = back_ref[:, place(k)]
            give_whole(far_ref, k, both[:32] + both[32:])


def join_kernel(whole_ref, low_ref, far_ref, near_ref, scale_ref, noise_ref, out_ref):
    pair = on_pair()
    lane = lax.broadcasted_iota(jnp.int32, (8, 128), 1)
    near = near_ref[:PEERS]
    sums = jnp.where(
        lane < 72,
        far_ref[PEERS] + near_ref[PEERS],
        jnp.where(lane < 100, scale_ref[0], noise_ref[0]),
    )
    out_ref[:, :8] = whole_ref[...] + jnp.where(pair, 0.0, near)
    out_ref[:, 8:] = low_ref[...] + jnp.where(pair, near, 0.0) + sums


def finish_kernel(got_ref, rhs_ref, sol_ref, res_ref):
    pair = got_ref[0, 8:]
    scale, noise = pair[0:1, 72:73], pair[0:1, 100:101]
    whole = [None] * GROUPS
    part = [None] * (2 * GROUPS)
    sums = got_ref[len(PAIRS), 8:]

    def plus(x, y):
        return y if x is None else x + y

    for k, (a, b, t) in enumerate(PAIRS):
        low = got_ref[k, 8:]
        whole[a] = plus(whole[a], got_ref[k, :8])
        part[2 * b + t] = plus(part[2 * b + t], low)
        sums = sums + low
    for a in range(GROUPS):
        whole[a] = plus(whole[a], got_ref[len(PAIRS) + a, :8])
        if a:
            sums = sums + got_ref[len(PAIRS) + a, 8:]
    mine = jnp.where(lax.axis_index("xh") == 0, sums[:, 64:68], sums[:, 68:72])
    product = jnp.concatenate([mine[:, 0:1], mine[:, 1:2]], axis=0)
    square = jnp.concatenate([mine[:, 2:3], mine[:, 3:4]], axis=0)
    step = square / (scale * product + noise * square)
    image = jnp.concatenate(
        [
            jnp.concatenate(
                [
                    x[:, 64 * m + 32 * h : 64 * m + 32 * h + 32]
                    for h in range(2)
                    for x in whole
                ],
                axis=1,
            )
            for m in range(2)
        ],
        axis=0,
    )
    blank = jnp.zeros((8, 16), F32)
    image = image + jnp.concatenate(
        [
            jnp.concatenate(
                [
                    blank if x is None else x[:, 32 * m + 16 * h : 32 * m + 16 * h + 16]
                    for h in range(2)
                    for x in part
                ],
                axis=1,
            )
            for m in range(2)
        ],
        axis=0,
    )
    direction = rhs_ref[...]
    sol_ref[...] = step * direction
    res_ref[...] = direction - step * (scale * image + noise * direction)


def on_device(encodings, first_weight, second_weight, inv_scale, outputscale, noise, rhs):
    hbm, vmem = pl.BlockSpec(memory_space=pltpu.HBM), pl.BlockSpec(memory_space=pltpu.VMEM)
    swap = [(0, 1), (1, 0)]
    sent = pl.pallas_call(
        pack_kernel,
        out_shape=pltpu.VMEM((PEERS, 24, 128), F32),
        in_specs=[hbm] * 5,
        scratch_shapes=[
            pltpu.VMEM(encodings.shape, BF16),
            pltpu.VMEM(first_weight.shape, BF16),
            pltpu.VMEM(second_weight.shape[::-1], BF16),
            pltpu.VMEM((1, inv_scale.size), F32),
            pltpu.VMEM(rhs.shape, F32),
            pltpu.VMEM((GROUPS, 16, 128), F32),
            pltpu.VMEM((2 * GROUPS, 8, 128), F32),
            pltpu.SemaphoreType.DMA((2 * STEPS,)),
            pltpu.SemaphoreType.DMA((3,)),
        ],
        name="features",
    )(encodings, first_weight, second_weight.T, inv_scale.reshape(1, -1), rhs)
    own = lax.all_to_all(sent, ("xh", "g"), 0, 0, tiled=True)
    other = lax.ppermute(own[:, 8:], "c", swap)
    cost = pl.CostEstimate(flops=4 << 30, bytes_accessed=1 << 20, transcendentals=1 << 21)
    *rows, back = pl.pallas_call(
        near_kernel,
        out_shape=(
            jax.ShapeDtypeStruct((2 * HALF, DEPTH), BF16),
            jax.ShapeDtypeStruct((TILES, 32, 128), F32),
            jax.ShapeDtypeStruct((64, 2 * HALF), BF16),
            jax.ShapeDtypeStruct((TILES, 32, 128), F32),
            jax.ShapeDtypeStruct((64, 2 * HALF), F32),
        ),
        scratch_shapes=[
            pltpu.VMEM((DEPTH, 2 * HALF), BF16),
            pltpu.VMEM((64, 2 * HALF), BF16),
        ],
        compiler_params=pltpu.CompilerParams(vmem_limit_bytes=24 << 20),
        cost_estimate=cost,
        name="own_columns",
    )(own)
    whole, low, far = pl.pallas_call(
        far_kernel,
        out_shape=tuple(jax.ShapeDtypeStruct((n, 8, 128), F32) for n in (PEERS, PEERS, PEERS + 1)),
        scratch_shapes=[
            pltpu.VMEM((DEPTH, 2 * HALF), BF16),
            pltpu.VMEM((64, 2 * HALF), BF16),
            pltpu.VMEM((64, 2 * HALF), F32),
        ],
        compiler_params=pltpu.CompilerParams(vmem_limit_bytes=24 << 20),
        cost_estimate=cost,
        name="other_columns",
    )(other, *rows, back)
    near = lax.ppermute(far, "c", swap)
    smem = pl.BlockSpec(memory_space=pltpu.SMEM)
    partial = pl.pallas_call(
        join_kernel,
        out_shape=jax.ShapeDtypeStruct((PEERS, 16, 128), F32),
        in_specs=[vmem] * 4 + [smem] * 2,
        compiler_params=pltpu.CompilerParams(vmem_limit_bytes=8 << 20),
        name="join",
    )(whole, low, far, near, outputscale, noise)
    got = lax.all_to_all(partial, ("xh", "g"), 0, 0, tiled=True)
    return pl.pallas_call(
        finish_kernel,
        out_shape=(jax.ShapeDtypeStruct(rhs.shape, F32),) * 2,
        in_specs=[vmem] * 2,
        compiler_params=pltpu.CompilerParams(vmem_limit_bytes=8 << 20),
        name="update",
    )(got, rhs)


def solution(mesh):
    split = Mesh(mesh.devices.reshape(CHIPS, 2, 2), ("g", "c", "xh"))
    vectors = P("xh", ("g", "c"))
    return jax.shard_map(
        on_device,
        mesh=split,
        in_specs=(P(("g", "c", "xh"), None), P(), P(), P(), P(), P(), vectors),
        out_specs=(vectors, vectors),
        check_vma=False,
    )
```
